256 devices in a mesh: det: 32 (over x, z), tile: 8 (over y, core).
Axes of the slice: x: 4, y: 4, z: 8, core: 2. Of those that a mesh axis runs over, the one named last changes fastest.
Arguments:
- detector_samples: float32 [128, 32768], P('det', 'tile'), may hold values from -180 to 180
- pixels: int32 [128, 32768], P('det', 'tile'), may hold values from 0 to 16383
- crossings: int32 [128, 8, 4], P('det', 'tile'), may hold values from 0 to 511, as said below
- lengths: int32 [128, 8, 16], P('det', 'tile'), may hold values from 1 to 512, 4096 in all within a row
- mode_templates: float32 [128, 64], replicated, may hold values from -0.5 to 0.5
- mixing: float32 [64, 64], replicated, may hold values from -0.2 to 1
- sky_map: float32 [512, 128, 128], P(('det', 'tile')), may hold values from -6 to 6
Outputs:
- sky_estimate: float32 [512, 128, 128], P(('det', 'tile'))
- baseline_fit: float32 [128, 8, 16], P('det', 'tile')
The draws below stay inside these ranges and needn't reach their ends.
Inputs may be any that keep to these rules, and one draw needn't show every extreme that they name: `crossings`: tile g is owned by device g // 2 of det+tile. In each time block, the entries of the 4 detectors of one det index name exactly 16 distinct tiles, owned by 16 different devices whose tile index is the block's, each tile named by exactly 1 of these entries.
All inputs are finite; a program needn't handle non-finite values.
Results may differ from the reference program's by a relative error of at most 0.0015.
Values may be sent and summed in bfloat16 or wider, within the bound.
A program may use at most 64 MiB of HBM per device.

```python
import math
import jax
import jax.numpy as jnp
import numpy as np
from jax import lax

SIDE = 128
PIX = 16384
TILE_DEV = 2
MODES = 64
DETECTORS_LOCAL = 4
SAMP_DEV = 4096
SEG_PER = 4
BASELINE_COUNT = 16
ITERS = 2
DETECTOR_COUNT = 128
TIME_BLOCKS = 8
SAMPLES = 32768
TILES = 512
NEED = 16


def draw_detector_samples(key, part):
    first, second = jax.random.split(key, 2)
    detector_scale = jnp.exp(jax.random.uniform(second, (DETECTOR_COUNT, 1), jnp.float32, 0.0, math.log(10.0)))
    ramp = 1.0 + 2.0 * jnp.arange(SAMPLES, dtype=jnp.float32)[None, :] / SAMPLES
    noise = jnp.clip(jax.random.normal(first, (DETECTOR_COUNT, SAMPLES), jnp.float32), -6.0, 6.0)
    values = noise * detector_scale * ramp
    return values


def draw_mixing(key, part):
    first, second = jax.random.split(key, 2)
    diagonal = jax.random.uniform(first, (MODES,), jnp.float32, 0.5, 1.0)
    spread = jnp.clip(jax.random.normal(second, (MODES, MODES), jnp.float32), -1.3, 1.3) * (1.2 / math.sqrt(MODES))
    spread = jnp.clip(spread, -0.2, 0.2)
    identity = jnp.eye(MODES, dtype=jnp.float32)
    return identity * diagonal[None, :] + spread * (1.0 - identity)


def draw_crossings(key, part):
    groups = DETECTOR_COUNT // DETECTORS_LOCAL
    first = jax.random.fold_in(key, 0)
    second = jax.random.fold_in(key, 1)
    fourth = jax.random.fold_in(key, 3)
    scores = jax.random.randint(first, (groups, TIME_BLOCKS, groups), 0, 1 << 20)
    owners = jnp.argsort(scores, axis=-1, stable=True)[:, :, :NEED].astype(jnp.int32)
    local_tile = jax.random.randint(second, (groups, TIME_BLOCKS, NEED), 0, TILE_DEV)
    block_index = jnp.arange(TIME_BLOCKS, dtype=jnp.int32)[None, :, None]
    tile_ids = (owners * TIME_BLOCKS + block_index) * TILE_DEV + local_tile
    entries = DETECTORS_LOCAL * SEG_PER
    repeats = entries // NEED
    every = jnp.broadcast_to(jnp.arange(entries, dtype=jnp.int32) // repeats, (groups, TIME_BLOCKS, entries))
    shuffle = jnp.argsort(jax.random.randint(fourth, (groups, TIME_BLOCKS, entries), 0, 1 << 20), axis=-1, stable=True)
    choose = jnp.take_along_axis(every, shuffle, axis=-1)
    chosen_entries = jnp.take_along_axis(tile_ids, choose, axis=-1)
    chosen_entries = chosen_entries.reshape(groups, TIME_BLOCKS, DETECTORS_LOCAL, SEG_PER).transpose(0, 2, 1, 3).reshape(DETECTOR_COUNT, TIME_BLOCKS, SEG_PER)
    return chosen_entries.astype(jnp.int32)


def set_ends(drawn, own_key, least, high):
    extent = drawn.shape
    spot = [jax.random.randint(jax.random.fold_in(own_key, axis), (), 0, extent[axis]) for axis in range(len(extent))]
    drawn = drawn.at[tuple(spot)].set(least)
    longest = extent.index(max(extent))
    spot[longest] = (spot[longest] + 1) % extent[longest]
    return drawn.at[tuple(spot)].set(high)


def level_of(rng, shape, pieces, low, top_value):
    loudness, own = 1.0, jax.random.fold_in(rng, 6)
    for dim, parts in pieces:
        heights = jnp.exp(jax.random.uniform(jax.random.fold_in(own, dim), (parts,), jnp.float32, low / len(pieces), top_value / len(pieces)))
        loudness = loudness * jnp.repeat(heights, shape[dim] // parts).reshape([-1 if axis == dim else 1 for axis in range(len(shape))])
    return loudness


def split_up(count, total, most, lean):
    loads = [(1 << 20) // math.isqrt(rank ** lean) + 1 for rank in range(2, count + 1)]
    rest, holding = total - most - (count - 1), [1] * (count - 1)
    while rest > 0:
        candidates = [i for i in range(count - 1) if holding[i] < most]
        whole, left = sum([loads[i] for i in candidates]), rest
        for i in candidates:
            more = min(most - holding[i], max(1, left * loads[i] // whole), rest)
            holding[i] = holding[i] + more
            rest = rest - more
    return np.array([most] + holding)


def uneven(key, amount, total, most, skew):
    if amount == 2:
        one = jax.random.randint(key, (), max(1, total - most), min(most, total - 1) + 1)
        return jnp.stack([one, total - one])
    sizes = jnp.asarray(split_up(amount, total, most, skew), jnp.int32)
    pairs = (amount - 1) // 2
    source_of, sink = sizes[1:1 + 2 * pairs:2], sizes[2:2 + 2 * pairs:2]
    margin = jnp.minimum(source_of - 1, most - sink)
    passed = jax.random.randint(jax.random.fold_in(key, 1), (pairs,), 0, 1 << 20) % (margin + 1)
    sizes = sizes.at[1:1 + 2 * pairs:2].set(source_of - passed).at[2:2 + 2 * pairs:2].set(sink + passed)
    return sizes[jax.random.permutation(jax.random.fold_in(key, 2), amount)]


def bell_draw(rng, extent, scale, reach, pieces=(), kind=jnp.bfloat16):
    gain = level_of(rng, extent, pieces, -0.22, 0.18) if pieces else 1.0
    drawn = jax.random.normal(rng, extent, jnp.float32) * scale * gain
    return jnp.minimum(jnp.maximum(drawn, -reach), reach).astype(kind)


def setup_inputs(seed: int = 0) -> dict:
    splits = jax.random.split(jax.random.key(seed), 8)
    return {
        "detector_samples": draw_detector_samples(jax.random.fold_in(splits[7], 71), 0),
        "pixels": set_ends(jax.random.randint(splits[1], (DETECTOR_COUNT, SAMPLES), 0, PIX), jax.random.fold_in(splits[1], 1), 0, PIX - 1).astype(jnp.int32),
        "crossings": draw_crossings(jax.random.fold_in(splits[7], 71), 0),
        "lengths": jax.vmap(lambda own: uneven(own, BASELINE_COUNT, SAMP_DEV, 2 * SAMP_DEV // BASELINE_COUNT, 2))(jax.random.split(splits[3], DETECTOR_COUNT * TIME_BLOCKS)).reshape((DETECTOR_COUNT, TIME_BLOCKS, BASELINE_COUNT)).astype(jnp.int32),
        "mode_templates": bell_draw(splits[4], (DETECTOR_COUNT, MODES), DETECTOR_COUNT ** -0.5, 0.5, (), jnp.float32),
        "mixing": draw_mixing(jax.random.fold_in(splits[7], 71), 0),
        "sky_map": bell_draw(splits[6], (TILES, SIDE, SIDE), 1.0, 6.0, ((0, 256),), jnp.float32),
    }


HUBER = 1.345
EPS = 1e-05

def reference(detector_samples, pixels, crossings, lengths, mode_templates, mixing, sky_map):
    part_length = SAMP_DEV // SEG_PER
    tile_of = jnp.repeat(crossings.reshape(DETECTOR_COUNT, TIME_BLOCKS * SEG_PER), part_length, axis=1).astype(jnp.int32)
    pixel_rows = (pixels // SIDE).astype(jnp.int32)
    pixel_cols = (pixels % SIDE).astype(jnp.int32)
    segment_ends = jnp.cumsum(lengths, axis=2).astype(jnp.int32).reshape(DETECTOR_COUNT * TIME_BLOCKS, BASELINE_COUNT)
    position = jnp.arange(SAMP_DEV, dtype=jnp.int32)
    local_segment = jax.vmap(lambda row_ends: jnp.searchsorted(row_ends, position, side='right'))(segment_ends).astype(jnp.int32)
    segment_index = (jnp.arange(DETECTOR_COUNT * TIME_BLOCKS, dtype=jnp.int32)[:, None] * BASELINE_COUNT + local_segment).reshape(DETECTOR_COUNT, SAMPLES)
    segment_flat = segment_index.reshape(-1)
    segment_total = DETECTOR_COUNT * TIME_BLOCKS * BASELINE_COUNT
    flat_pixel = (tile_of * PIX + pixels).astype(jnp.int32).reshape(-1)
    current_estimate = sky_map
    baseline_values = jnp.zeros((segment_total,), jnp.float32)
    for iteration in range(ITERS):
        rounded = lax.optimization_barrier(current_estimate.astype(jnp.bfloat16)).astype(jnp.float32)
        pointed_pixels = rounded[tile_of, pixel_rows, pixel_cols]
        residual_signal = detector_samples - pointed_pixels - baseline_values[segment_index]
        projected = jnp.dot(mode_templates.T, residual_signal, precision=lax.Precision.HIGHEST)
        amplitudes = jnp.dot(mixing, projected, precision=lax.Precision.HIGHEST)
        cleaned = residual_signal - jnp.dot(mode_templates, amplitudes, precision=lax.Precision.HIGHEST)
        noise = jnp.sqrt(lax.optimization_barrier(jnp.sum(cleaned * cleaned, axis=1, keepdims=True)) / SAMPLES + EPS)
        weight = HUBER * noise / jnp.maximum(jnp.abs(cleaned), HUBER * noise)
        numerator = jax.ops.segment_sum((weight * cleaned).reshape(-1), segment_flat, segment_total)
        denominator = jax.ops.segment_sum(weight.reshape(-1), segment_flat, segment_total)
        baseline_step = numerator / denominator
        baseline_values = baseline_values + baseline_step
        remainder = cleaned - baseline_step[segment_index]
        value_sums = jnp.zeros((TILES * PIX,), jnp.float32).at[flat_pixel].add((weight * remainder).reshape(-1))
        weight_sums = jnp.zeros((TILES * PIX,), jnp.float32).at[flat_pixel].add(weight.reshape(-1))
        current_estimate = current_estimate + (value_sums / jnp.maximum(weight_sums, 1.0)).reshape(TILES, SIDE, SIDE)
    return (current_estimate, baseline_values.reshape(DETECTOR_COUNT, TIME_BLOCKS, BASELINE_COUNT))
```

```python
import functools

import jax
import jax.numpy as jnp
from jax import lax
from jax.experimental import pallas as pl
from jax.experimental.pallas import tpu as pltpu
from jax.sharding import PartitionSpec as P

SIDE = 128
PIX = 16384
TILE_DEV = 2
MODES = 64
DETECTORS_LOCAL = 4
SAMP_DEV = 4096
SEG_PER = 4
BASELINE_COUNT = 16
ITERS = 2
PART = SAMP_DEV // SEG_PER
ENTRIES = DETECTORS_LOCAL * SEG_PER
LANES = 128
COLS = 256
ROWS = PIX * TILE_DEV // COLS

HUBER = 1.345
EPS = 1e-05
MESH = pl.DeviceIdType.MESH
ZRING = 8


def kernel(
    groups,
    blocks,
    ent_ref,
    own_ref,
    det_ref,
    code_ref,
    ends_ref,
    templ_ref,
    mixing_ref,
    sky_ref,
    sky_out,
    base_out,
    code_h,
    det_h,
    seg_h,
    code_e,
    val_e,
    work,
    clean_h,
    stack,
    matrix,
    current,
    acc,
    lhs,
    coloh,
    rowoh,
    send_i,
    recv_i,
    send_a,
    recv_a,
    send_b,
    recv_b,
    send_c,
    recv_c,
    send_d,
    recv_d,
    send_e,
    recv_e,
    sent,
    sem_i,
    sem_a,
    sem_b,
    sem_c,
    sem_d,
    sem_e,
):
    me = lax.axis_index("det")
    block = lax.axis_index("tile")
    chunks = SAMP_DEV // LANES
    xring = groups // ZRING
    my_x, my_z = me // ZRING, me % ZRING

    def peer(step):
        x = (my_x + step // ZRING) % xring
        z = (my_z + step % ZRING) % ZRING
        return x * ZRING + z

    def copy_to(src, dst, send_sem, recv_sem, **place):
        return pltpu.make_async_remote_copy(
            src_ref=src, dst_ref=dst, send_sem=send_sem, recv_sem=recv_sem,
            device_id=place, device_id_type=MESH,
        )

    def wait_bytes(ref, count, sem):
        view = ref.at[pl.ds(0, count)]
        pltpu.make_async_copy(view, view, sem).wait()

    barrier = pltpu.get_barrier_semaphore()

    def greet(step, carry):
        pl.semaphore_signal(barrier, inc=1, device_id={"det": peer(step)}, device_id_type=MESH)
        return carry

    lax.fori_loop(1, groups, greet, 0)

    def greet_tile(step, carry):
        pl.semaphore_signal(
            barrier, inc=1, device_id={"tile": (block + step) % blocks}, device_id_type=MESH
        )
        return carry

    lax.fori_loop(1, blocks, greet_tile, 0)

    det_h[...] = jnp.zeros_like(det_h)
    code_h[...] = jnp.zeros_like(code_h)
    clean_h[...] = jnp.zeros_like(clean_h)
    stack[...] = jnp.zeros_like(stack)
    for j in range(chunks):
        det_h[8 * j : 8 * j + DETECTORS_LOCAL, :] = det_ref[:, LANES * j : LANES * (j + 1)]
        code_h[8 * j : 8 * j + DETECTORS_LOCAL, :] = code_ref[:, LANES * j : LANES * (j + 1)]

    def entry_rows(e):
        l, k = e // SEG_PER, e % SEG_PER
        return pl.ds(8 * (PART // LANES) * k + l, PART // LANES, stride=8)

    for e in range(ENTRIES):
        code_e[e] = code_h[entry_rows(e), :]

    def pack_codes(o, carry):
        e = ent_ref[o]
        rows = code_e[jnp.maximum(e, 0)]
        send_i[o] = jnp.where(jnp.full(rows.shape, e, jnp.int32) >= 0, rows, -1)
        return carry

    lax.fori_loop(0, groups, pack_codes, 0)
    recv_i[me] = send_i[me]

    pl.semaphore_wait(barrier, groups - 1 + blocks - 1)

    def send_codes(step, carry):
        o = peer(step)
        copy_to(send_i.at[o], recv_i.at[me], sent.at[0], sem_i.at[me], det=o).start()
        return carry

    lax.fori_loop(1, groups, send_codes, 0)

    even = sky_ref[pl.ds(0, ROWS, stride=2), :]
    odd = sky_ref[pl.ds(1, ROWS, stride=2), :]
    current[:, 0:LANES] = even
    current[:, LANES:COLS] = odd
    mixed = jnp.dot(
        templ_ref[...], mixing_ref[...],
        precision=lax.Precision.HIGHEST, preferred_element_type=jnp.float32,
    )
    matrix[...] = lax.dot_general(
        mixed, templ_ref[...], (((1,), (1,)), ((), ())),
        precision=lax.Precision.HIGHEST, preferred_element_type=jnp.float32,
    )
    home = (chunks, 8, LANES)
    position = (
        lax.broadcasted_iota(jnp.int32, home, 0) * LANES + lax.broadcasted_iota(jnp.int32, home, 2)
    )
    ends = ends_ref[...]
    seg = jnp.zeros(home, jnp.int32)
    for n in range(BASELINE_COUNT):
        seg += (position >= ends[:, n : n + 1][None]).astype(jnp.int32)
    seg_h[...] = seg.reshape(8 * chunks, LANES)

    baseline = [jnp.zeros((8, 1), jnp.float32) for _ in range(BASELINE_COUNT)]

    for it in range(ITERS):
        base_sem = 1 + 5 * it
        table = current[...].astype(jnp.bfloat16)

        def answer(step, carry):
            d = peer(step)
            if it == 0:
                @pl.when(step > 0)
                def _():
                    copy_to(send_i.at[d], recv_i.at[d], sent.at[0], sem_i.at[d], det=d).wait_recv()

                code = recv_i[d]
                for q in range(PART // LANES):
                    here = pl.ds(LANES * q, LANES)
                    row = lax.shift_right_arithmetic(code[q : q + 1, :], 8)
                    col = jnp.bitwise_and(code[q : q + 1, :], COLS - 1)
                    coloh[d, :, here] = (
                        jnp.broadcast_to(col, (COLS, LANES))
                        == lax.broadcasted_iota(jnp.int32, (COLS, LANES), 0)
                    ).astype(jnp.float32).astype(jnp.bfloat16)
                    rowoh[d, :, here] = (
                        jnp.broadcast_to(row, (ROWS, LANES))
                        == lax.broadcasted_iota(jnp.int32, (ROWS, LANES), 0)
                    ).astype(jnp.float32).astype(jnp.bfloat16)
            picked = jnp.dot(table, coloh[d], preferred_element_type=jnp.float32)
            picked = jnp.sum(picked * rowoh[d].astype(jnp.float32), axis=0, keepdims=True)
            rows = jnp.concatenate(
                [picked[:, LANES * q : LANES * (q + 1)] for q in range(PART // LANES)], axis=0
            )
            send_a[it, d] = rows.astype(jnp.bfloat16)

            @pl.when(step > 0)
            def _():
                copy_to(
                    send_a.at[it, d], recv_a.at[it, me], sent.at[base_sem], sem_a.at[it], det=d
                ).start()

            return carry

        lax.fori_loop(0, groups, answer, 0)
        recv_a[it, me] = send_a[it, me]
        wait_bytes(recv_a.at[it], groups - 1, sem_a.at[it])

        for e in range(ENTRIES):
            work[entry_rows(e), :] = recv_a[it, own_ref[e]].astype(jnp.float32)
        residual = det_h[...] - work[...]
        det_h_value = residual
        for j in range(chunks):
            send_b[it, j] = det_h_value[8 * j : 8 * j + DETECTORS_LOCAL, :]
        recv_b[it, me] = send_b[it, me]

        def send_pieces(step, carry):
            j = peer(step)
            copy_to(
                send_b.at[it, j], recv_b.at[it, me], sent.at[base_sem + 1], sem_b.at[it], det=j
            ).start()
            return carry

        lax.fori_loop(1, groups, send_pieces, 0)
        wait_bytes(recv_b.at[it], groups - 1, sem_b.at[it])

        for d in range(groups):
            stack[8 * d : 8 * d + DETECTORS_LOCAL, :] = recv_b[it, d]
        every = stack[...]
        every = every - jnp.dot(
            matrix[...], every,
            precision=lax.Precision.HIGHEST, preferred_element_type=jnp.float32,
        )
        for d in range(groups):
            send_c[it, d] = every[8 * d : 8 * d + DETECTORS_LOCAL, :]
        recv_c[it, me] = send_c[it, me]

        def send_cleaned(step, carry):
            d = peer(step)
            copy_to(
                send_c.at[it, d], recv_c.at[it, me], sent.at[base_sem + 2], sem_c.at[it], det=d
            ).start()
            return carry

        lax.fori_loop(1, groups, send_cleaned, 0)
        wait_bytes(recv_c.at[it], groups - 1, sem_c.at[it])

        for j in range(chunks):
            clean_h[8 * j : 8 * j + DETECTORS_LOCAL, :] = recv_c[it, j]
        cleaned = clean_h[...].reshape(home)
        send_d[it] = jnp.sum(cleaned * cleaned, axis=0)
        recv_d[it, block] = send_d[it]

        def send_squares(step, carry):
            b = (block + step) % blocks
            copy_to(
                send_d.at[it], recv_d.at[it, block], sent.at[base_sem + 3], sem_d.at[it], tile=b
            ).start()
            return carry

        lax.fori_loop(1, blocks, send_squares, 0)
        wait_bytes(recv_d.at[it], blocks - 1, sem_d.at[it])
        squares = jnp.sum(jnp.sum(recv_d[it], axis=0), axis=1, keepdims=True)
        level = HUBER * jnp.sqrt(squares / (SAMP_DEV * blocks) + EPS)
        weight = level[None] / jnp.maximum(jnp.abs(cleaned), level[None])
        weighted = weight * cleaned
        seg = seg_h[...].reshape(home)
        stepped = jnp.zeros(home, jnp.float32)
        for n in range(BASELINE_COUNT):
            inside = seg == n
            numerator = jnp.sum(
                jnp.sum(jnp.where(inside, weighted, 0.0), axis=0), axis=1, keepdims=True
            )
            denominator = jnp.sum(
                jnp.sum(jnp.where(inside, weight, 0.0), axis=0), axis=1, keepdims=True
            )
            increment = numerator / jnp.where(denominator > 0.0, denominator, 1.0)
            baseline[n] = baseline[n] + increment
            stepped = jnp.where(inside, increment[None], stepped)
        if it + 1 < ITERS:
            det_h[...] = det_h[...] - stepped.reshape(8 * chunks, LANES)
        work[...] = (weight * (cleaned - stepped)).reshape(8 * chunks, LANES)
        clean_h[...] = weight.reshape(8 * chunks, LANES)
        half = PART // LANES
        for e in range(ENTRIES):
            val_e[e, 0:half, :] = work[entry_rows(e), :]
            val_e[e, half : 2 * half, :] = clean_h[entry_rows(e), :]

        def pack_values(o, carry):
            send_e[it, o] = val_e[jnp.maximum(ent_ref[o], 0)]
            return carry

        lax.fori_loop(0, groups, pack_values, 0)
        recv_e[it, me] = send_e[it, me]

        def send_values(step, carry):
            o = peer(step)
            copy_to(
                send_e.at[it, o], recv_e.at[it, me], sent.at[base_sem + 4], sem_e.at[it, me], det=o
            ).start()
            return carry

        lax.fori_loop(1, groups, send_values, 0)
        clean_h[...] = jnp.zeros_like(clean_h)
        acc[...] = jnp.zeros_like(acc)

        def collect(step, carry):
            d = peer(step)

            @pl.when(step > 0)
            def _():
                copy_to(
                    send_e.at[it, d], recv_e.at[it, d], sent.at[base_sem + 4], sem_e.at[it, d], det=d
                ).wait_recv()

            pair = recv_e[it, d]
            high = pair.astype(jnp.bfloat16).astype(jnp.float32)
            low = pair - high
            for q in range(half):
                here = pl.ds(LANES * q, LANES)
                flags = rowoh[d, :, here].astype(jnp.float32)
                for t, term in enumerate(
                    (high[q : q + 1], low[q : q + 1], high[half + q : half + q + 1],
                     low[half + q : half + q + 1])
                ):
                    lhs[ROWS * t : ROWS * (t + 1), here] = (
                        flags * jnp.broadcast_to(term, (ROWS, LANES))
                    ).astype(jnp.bfloat16)
            acc[...] += lax.dot_general(
                lhs[...], coloh[d], (((1,), (1,)), ((), ())), preferred_element_type=jnp.float32
            )
            return carry

        lax.fori_loop(0, groups, collect, 0)
        values = acc[0:ROWS, :] + acc[ROWS : 2 * ROWS, :]
        weights = acc[2 * ROWS : 3 * ROWS, :] + acc[3 * ROWS : 4 * ROWS, :]
        current[...] = current[...] + values / jnp.maximum(weights, 1.0)

    sky_out[pl.ds(0, ROWS, stride=2), :] = current[:, 0:LANES]
    sky_out[pl.ds(1, ROWS, stride=2), :] = current[:, LANES:COLS]
    lane = lax.broadcasted_iota(jnp.int32, (8, LANES), 1)
    fit = jnp.zeros((8, LANES), jnp.float32)
    for n in range(BASELINE_COUNT):
        fit = jnp.where(lane == n, baseline[n], fit)
    base_out[...] = fit

    wait_bytes(send_i, groups - 1, sent.at[0])
    for it in range(ITERS):
        base_sem = 1 + 5 * it
        wait_bytes(send_a.at[it], groups - 1, sent.at[base_sem])
        wait_bytes(send_b.at[it], groups - 1, sent.at[base_sem + 1])
        wait_bytes(send_c.at[it], groups - 1, sent.at[base_sem + 2])
        wait_bytes(recv_d.at[it], blocks - 1, sent.at[base_sem + 3])
        wait_bytes(send_e.at[it], groups - 1, sent.at[base_sem + 4])


def local(detector_samples, pixels, crossings, lengths, mode_templates, mixing, sky_map):
    groups = lax.axis_size("det")
    blocks = lax.axis_size("tile")
    chunks = SAMP_DEV // LANES
    tile_ids = crossings.reshape(ENTRIES)
    owner = tile_ids // TILE_DEV // blocks
    matches = owner[None, :] == jnp.arange(groups, dtype=jnp.int32)[:, None]
    entry = jnp.max(
        jnp.where(matches, jnp.arange(ENTRIES, dtype=jnp.int32)[None, :], -1), axis=1
    )
    local_tile = crossings.reshape(DETECTORS_LOCAL, SEG_PER) % TILE_DEV
    codes = (
        pixels.reshape(DETECTORS_LOCAL, SEG_PER, PART) + (local_tile * PIX)[:, :, None]
    ).reshape(DETECTORS_LOCAL, SAMP_DEV)
    ends = jnp.cumsum(lengths.reshape(DETECTORS_LOCAL, BASELINE_COUNT), axis=1)
    ends = jnp.pad(ends, ((0, 8 - DETECTORS_LOCAL), (0, LANES - BASELINE_COUNT)))
    templates = jnp.pad(
        mode_templates.reshape(groups, DETECTORS_LOCAL, MODES),
        ((0, 0), (0, 8 - DETECTORS_LOCAL), (0, 0)),
    ).reshape(groups * 8, MODES)

    vmem = pl.BlockSpec(memory_space=pltpu.VMEM)
    smem = pl.BlockSpec(memory_space=pltpu.SMEM)
    f32, bf16, i32 = jnp.float32, jnp.bfloat16, jnp.int32
    dma = pltpu.SemaphoreType.DMA
    half = PART // LANES
    sky, fit = pl.pallas_call(
        functools.partial(kernel, groups, blocks),
        out_shape=(
            jax.ShapeDtypeStruct((TILE_DEV * SIDE, SIDE), f32),
            jax.ShapeDtypeStruct((8, LANES), f32),
        ),
        in_specs=[smem, smem] + [vmem] * 6,
        out_specs=(vmem, vmem),
        scratch_shapes=[
            pltpu.VMEM((8 * chunks, LANES), i32),
            pltpu.VMEM((8 * chunks, LANES), f32),
            pltpu.VMEM((8 * chunks, LANES), i32),
            pltpu.VMEM((ENTRIES, half, LANES), i32),
            pltpu.VMEM((ENTRIES, 2 * half, LANES), f32),
            pltpu.VMEM((8 * chunks, LANES), f32),
            pltpu.VMEM((8 * chunks, LANES), f32),
            pltpu.VMEM((8 * groups, LANES), f32),
            pltpu.VMEM((8 * groups, 8 * groups), f32),
            pltpu.VMEM((ROWS, COLS), f32),
            pltpu.VMEM((4 * ROWS, COLS), f32),
            pltpu.VMEM((4 * ROWS, PART), bf16),
            pltpu.VMEM((groups, COLS, PART), bf16),
            pltpu.VMEM((groups, ROWS, PART), bf16),
            pltpu.VMEM((groups, half, LANES), i32),
            pltpu.VMEM((groups, half, LANES), i32),
            pltpu.VMEM((ITERS, groups, half, LANES), bf16),
            pltpu.VMEM((ITERS, groups, half, LANES), bf16),
            pltpu.VMEM((ITERS, chunks, DETECTORS_LOCAL, LANES), f32),
            pltpu.VMEM((ITERS, groups, DETECTORS_LOCAL, LANES), f32),
            pltpu.VMEM((ITERS, groups, DETECTORS_LOCAL, LANES), f32),
            pltpu.VMEM((ITERS, chunks, DETECTORS_LOCAL, LANES), f32),
            pltpu.VMEM((ITERS, 8, LANES), f32),
            pltpu.VMEM((ITERS, blocks, 8, LANES), f32),
            pltpu.VMEM((ITERS, groups, 2 * half, LANES), f32),
            pltpu.VMEM((ITERS, groups, 2 * half, LANES), f32),
            dma((1 + 5 * ITERS,)),
            dma((groups,)),
            dma((ITERS,)),
            dma((ITERS,)),
            dma((ITERS,)),
            dma((ITERS,)),
            dma((ITERS, groups)),
        ],
        compiler_params=pltpu.CompilerParams(
            collective_id=0, has_side_effects=True, vmem_limit_bytes=60 * 1024 * 1024
        ),
    )(entry, owner, detector_samples, codes, ends, templates, mixing,
      sky_map.reshape(TILE_DEV * SIDE, SIDE))
    return (
        sky.reshape(TILE_DEV, SIDE, SIDE),
        fit[:DETECTORS_LOCAL, :BASELINE_COUNT].reshape(DETECTORS_LOCAL, 1, BASELINE_COUNT),
    )


def solution(mesh):
    placed = (
        P("det", "tile"),
        P("det", "tile"),
        P("det", "tile", None),
        P("det", "tile", None),
        P(),
        P(),
        P(("det", "tile"), None, None),
    )
    return jax.shard_map(
        local,
        mesh=mesh,
        in_specs=placed,
        out_specs=(P(("det", "tile"), None, None), P("det", "tile", None)),
        check_vma=False,
    )
```

```python
import functools

import jax
import jax.numpy as jnp
from jax import lax
from jax.experimental import pallas as pl
from jax.experimental.pallas import tpu as pltpu
from jax.sharding import PartitionSpec as P

SIDE = 128
PIX = 16384
TILE_DEV = 2
MODES = 64
DETECTORS_LOCAL = 4
SAMP_DEV = 4096
SEG_PER = 4
BASELINE_COUNT = 16
ITERS = 2
PART = SAMP_DEV // SEG_PER
ENTRIES = DETECTORS_LOCAL * SEG_PER
LANES = 128
COLS = 256
ROWS = PIX // COLS
HALF = PART // LANES
TERMS = 3
TOGETHER = 4

HUBER = 1.345
EPS = 1e-05
MESH = pl.DeviceIdType.MESH
ZRING = 8


def kernel(
    groups,
    blocks,
    cross_ref,
    len_ref,
    det_hbm,
    pix_hbm,
    templ_hbm,
    mixing_hbm,
    sky_hbm,
    sky_out,
    base_out,
    det_ref,
    pix_ref,
    templ_ref,
    mixing_ref,
    current,
    ent_ref,
    templ_h,
    code_h,
    det_h,
    seg_h,
    code_e,
    val_e,
    work,
    clean_h,
    stack,
    matrix,
    table,
    chosen,
    parts,
    acc,
    coloh,
    rowoh,
    send_i,
    recv_i,
    send_a,
    recv_a,
    send_b,
    recv_b,
    send_c,
    recv_c,
    send_d,
    recv_d,
    send_e,
    recv_e,
    load_sem,
    sent,
    sem_i,
    sem_a,
    sem_b,
    sem_c,
    sem_d,
    sem_e,
):
    me = lax.axis_index("det")
    block = lax.axis_index("tile")
    chunks = SAMP_DEV // LANES
    xring = groups // ZRING
    my_x, my_z = lax.div(me, ZRING), lax.rem(me, ZRING)

    loads = [
        pltpu.make_async_copy(src, dst, load_sem.at[i])
        for i, (src, dst) in enumerate(
            ((pix_hbm, pix_ref), (det_hbm, det_ref), (templ_hbm, templ_ref),
             (mixing_hbm, mixing_ref), (sky_hbm, current))
        )
    ]
    for load in loads:
        load.start()

    def hops(dx, dz):
        return min(dx, xring - dx) + min(dz, ZRING - dz)

    xs = [lax.rem(my_x + dx, xring) * ZRING for dx in range(xring)]
    zs = [lax.rem(my_z + dz, ZRING) for dz in range(ZRING)]
    offsets = sorted(
        ((dx, dz) for dx in range(xring) for dz in range(ZRING) if dx or dz), key=lambda o: hops(*o)
    )
    near = [xs[dx] + zs[dz] for dx, dz in offsets]
    far = near[::-1]

    def copy_to(src, dst, send_sem, recv_sem, **place):
        return pltpu.make_async_remote_copy(
            src_ref=src, dst_ref=dst, send_sem=send_sem, recv_sem=recv_sem,
            device_id=place, device_id_type=MESH,
        )

    def wait_bytes(ref, count, sem):
        view = ref.at[pl.ds(0, count)]
        pltpu.make_async_copy(view, view, sem).wait()

    barrier = pltpu.get_barrier_semaphore()
    for o in far:
        pl.semaphore_signal(barrier, inc=1, device_id={"det": o}, device_id_type=MESH)
    others = [lax.rem(block + step, blocks) for step in range(1, blocks)]
    for b in others:
        pl.semaphore_signal(barrier, inc=1, device_id={"tile": b}, device_id_type=MESH)

    def entry_place(e):
        return e // SEG_PER, e % SEG_PER

    tiles = [cross_ref[entry_place(e)[0], 0, entry_place(e)[1]] for e in range(ENTRIES)]
    owners = [lax.div(tile, TILE_DEV * blocks) for tile in tiles]

    def find_entry(o, carry):
        found = jnp.int32(-1)
        for e in range(ENTRIES):
            found = jnp.where(owners[e] == o, e, found)
        ent_ref[o] = found
        return carry

    lax.fori_loop(0, groups, find_entry, 0)

    det_h[...] = jnp.zeros_like(det_h)
    code_h[...] = jnp.zeros_like(code_h)
    clean_h[...] = jnp.zeros_like(clean_h)
    stack[...] = jnp.zeros_like(stack)
    templ_h[...] = jnp.zeros_like(templ_h)
    loads[0].wait()
    for j in range(chunks):
        code_h[8 * j : 8 * j + DETECTORS_LOCAL, :] = pix_ref[:, LANES * j : LANES * (j + 1)]

    def entry_rows(e):
        l, k = entry_place(e)
        return pl.ds(8 * HALF * k + l, HALF, stride=8)

    for e in range(ENTRIES):
        code_e[e] = code_h[entry_rows(e), :] + lax.rem(tiles[e], TILE_DEV) * PIX

    def pack_codes(o, carry):
        e = ent_ref[o]
        rows = code_e[jnp.maximum(e, 0)]
        send_i[o] = jnp.where(jnp.full(rows.shape, e, jnp.int32) >= 0, rows, -1)
        return carry

    lax.fori_loop(0, groups, pack_codes, 0)
    recv_i[me] = send_i[me]
    for load in loads[1:]:
        load.wait()

    pl.semaphore_wait(barrier, groups - 1 + blocks - 1)
    for o in far:
        copy_to(send_i.at[o], recv_i.at[me], sent.at[0], sem_i.at[me], det=o).start()

    for j in range(chunks):
        det_h[8 * j : 8 * j + DETECTORS_LOCAL, :] = det_ref[:, LANES * j : LANES * (j + 1)]
    table[...] = current[...].astype(jnp.bfloat16).astype(jnp.float32)
    for d in range(groups):
        templ_h[8 * d : 8 * d + DETECTORS_LOCAL, :] = templ_ref[
            DETECTORS_LOCAL * d : DETECTORS_LOCAL * (d + 1), :
        ]
    mixed = jnp.dot(
        templ_h[...], mixing_ref[...],
        precision=lax.Precision.HIGHEST, preferred_element_type=jnp.float32,
    )
    matrix[...] = lax.dot_general(
        mixed, templ_h[...], (((1,), (1,)), ((), ())),
        precision=lax.Precision.HIGHEST, preferred_element_type=jnp.float32,
    )
    home = (chunks, 8, LANES)
    position = (
        lax.broadcasted_iota(jnp.int32, home, 0) * LANES + lax.broadcasted_iota(jnp.int32, home, 2)
    )
    sublane = lax.broadcasted_iota(jnp.int32, (8, LANES), 0)
    ends = [jnp.int32(0)] * DETECTORS_LOCAL
    seg = jnp.zeros(home, jnp.int32)
    for n in range(BASELINE_COUNT):
        end = jnp.zeros((8, LANES), jnp.int32)
        for l in range(DETECTORS_LOCAL):
            ends[l] = ends[l] + len_ref[l, 0, n]
            end = jnp.where(sublane == l, ends[l], end)
        seg += (position >= end[None]).astype(jnp.int32)
    seg_h[...] = seg.reshape(8 * chunks, LANES)

    def flags(first, last):
        def one(d, carry):
            code = recv_i[d]
            row = jnp.where(
                code < 0, -1, jnp.bitwise_and(lax.shift_right_arithmetic(code, 8), ROWS - 1)
            )
            col = jnp.bitwise_and(code, COLS - 1)
            for q in range(HALF):
                coloh[d, q] = (
                    jnp.broadcast_to(col[q : q + 1, :], (COLS, LANES))
                    == lax.broadcasted_iota(jnp.int32, (COLS, LANES), 0)
                ).astype(jnp.float32).astype(jnp.bfloat16)
                rowoh[d, q] = (
                    jnp.broadcast_to(row[q : q + 1, :], (ROWS, LANES))
                    == lax.broadcasted_iota(jnp.int32, (ROWS, LANES), 0)
                ).astype(jnp.float32).astype(jnp.bfloat16)
            return carry

        lax.fori_loop(first, last, one, 0)

    def peer_of(step):
        x = lax.rem(my_x + lax.div(step, ZRING), xring)
        z = lax.rem(my_z + lax.rem(step, ZRING), ZRING)
        return x * ZRING + z

    baseline = [jnp.zeros((8, 1), jnp.float32) for _ in range(BASELINE_COUNT)]

    for it in range(ITERS):
        base_sem = 1 + 5 * it

        def answer(batch, carry):
            slots = [
                peer_of(step if it == 0 else lax.rem(step + 20, groups))
                for step in (TOGETHER * batch + i for i in range(TOGETHER))
            ]
            if it == 0:
                for i, d in enumerate(slots):
                    @pl.when(TOGETHER * batch + i > 0)
                    def _():
                        copy_to(
                            send_i.at[d], recv_i.at[d], sent.at[0], sem_i.at[d], det=d
                        ).wait_recv()
            values = []
            for i, d in enumerate(slots):
                code = recv_i[d]
                row = jnp.bitwise_and(lax.shift_right_arithmetic(code, 7), SIDE - 1)
                col = jnp.bitwise_and(code, LANES - 1)
                second = code >= PIX
                for g in range(SIDE // 8):
                    chosen[i, 8 * g : 8 * g + 8, :] = jnp.where(
                        second,
                        table[SIDE + 8 * g : SIDE + 8 * g + 8, :],
                        table[8 * g : 8 * g + 8, :],
                    )
                value = jnp.zeros((HALF, LANES), jnp.float32)
                for r in range(SIDE):
                    line = jnp.broadcast_to(chosen[i, r : r + 1, :], (HALF, LANES))
                    value = jnp.where(row == r, jnp.take_along_axis(line, col, axis=1), value)
                values.append(value)
            for d, value in zip(slots, values):
                send_a[it, d] = value.astype(jnp.bfloat16)
            for d in slots:
                @pl.when(d != me)
                def _():
                    copy_to(
                        send_a.at[it, d], recv_a.at[it, me], sent.at[base_sem], sem_a.at[it], det=d
                    ).start()

            return carry

        lax.fori_loop(0, groups // TOGETHER, answer, 0)
        recv_a[it, me] = send_a[it, me]
        if it == 0:
            flags(0, groups // 2)
        wait_bytes(recv_a.at[it], groups - 1, sem_a.at[it])

        for e in range(ENTRIES):
            work[entry_rows(e), :] = recv_a[it, owners[e]].astype(jnp.float32)
        residual = det_h[...] - work[...]
        for j in range(chunks):
            send_b[it, j] = residual[8 * j : 8 * j + DETECTORS_LOCAL, :]
        recv_b[it, me] = send_b[it, me]
        for j in far:
            copy_to(
                send_b.at[it, j], recv_b.at[it, me], sent.at[base_sem + 1], sem_b.at[it], det=j
            ).start()
        if it == 0:
            flags(groups // 2, groups)
        wait_bytes(recv_b.at[it], groups - 1, sem_b.at[it])

        for d in range(groups):
            stack[8 * d : 8 * d + DETECTORS_LOCAL, :] = recv_b[it, d]
        every = stack[...]
        every = every - jnp.dot(
            matrix[...], every,
            precision=lax.Precision.HIGHEST, preferred_element_type=jnp.float32,
        )
        for d in range(groups):
            send_c[it, d] = every[8 * d : 8 * d + DETECTORS_LOCAL, :]
        recv_c[it, me] = send_c[it, me]
        for d in far:
            copy_to(
                send_c.at[it, d], recv_c.at[it, me], sent.at[base_sem + 2], sem_c.at[it], det=d
            ).start()
        acc[...] = jnp.zeros_like(acc)
        wait_bytes(recv_c.at[it], groups - 1, sem_c.at[it])

        for j in range(chunks):
            clean_h[8 * j : 8 * j + DETECTORS_LOCAL, :] = recv_c[it, j]
        cleaned = clean_h[...].reshape(home)
        send_d[it] = jnp.sum(cleaned * cleaned, axis=0)
        recv_d[it, block] = send_d[it]
        for b in others:
            copy_to(
                send_d.at[it], recv_d.at[it, block], sent.at[base_sem + 3], sem_d.at[it], tile=b
            ).start()
        wait_bytes(recv_d.at[it], blocks - 1, sem_d.at[it])
        squares = jnp.sum(jnp.sum(recv_d[it], axis=0), axis=1, keepdims=True)
        level = HUBER * jnp.sqrt(squares / (SAMP_DEV * blocks) + EPS)
        weight = level[None] / jnp.maximum(jnp.abs(cleaned), level[None])
        weighted = weight * cleaned
        seg = seg_h[...].reshape(home)
        stepped = jnp.zeros(home, jnp.float32)
        for n in range(BASELINE_COUNT):
            inside = seg == n
            numerator = jnp.sum(
                jnp.sum(jnp.where(inside, weighted, 0.0), axis=0), axis=1, keepdims=True
            )
            denominator = jnp.sum(
                jnp.sum(jnp.where(inside, weight, 0.0), axis=0), axis=1, keepdims=True
            )
            increment = numerator / jnp.where(denominator > 0.0, denominator, 1.0)
            baseline[n] = baseline[n] + increment
            stepped = jnp.where(inside, increment[None], stepped)
        if it + 1 < ITERS:
            det_h[...] = det_h[...] - stepped.reshape(8 * chunks, LANES)
        work[...] = (weight * (cleaned - stepped)).reshape(8 * chunks, LANES)
        clean_h[...] = weight.reshape(8 * chunks, LANES)
        for e in range(ENTRIES):
            value = work[entry_rows(e), :]
            high = value.astype(jnp.bfloat16)
            val_e[e, 0] = high
            val_e[e, 1] = (value - high.astype(jnp.float32)).astype(jnp.bfloat16)
            val_e[e, 2] = clean_h[entry_rows(e), :].astype(jnp.bfloat16)

        for o in far:
            send_e[it, o] = val_e[jnp.maximum(ent_ref[o], 0)]
            copy_to(
                send_e.at[it, o], recv_e.at[it, me], sent.at[base_sem + 4], sem_e.at[it, me], det=o
            ).start()
        recv_e[it, me] = val_e[jnp.maximum(ent_ref[me], 0)]
        clean_h[...] = jnp.zeros_like(clean_h)

        def collect(batch, carry):
            slots = [peer_of(TOGETHER * batch + i) for i in range(TOGETHER)]
            for i, d in enumerate(slots):
                @pl.when(TOGETHER * batch + i > 0)
                def _():
                    copy_to(
                        send_e.at[it, d], recv_e.at[it, d], sent.at[base_sem + 4], sem_e.at[it, d],
                        det=d,
                    ).wait_recv()
            for i, d in enumerate(slots):
                for t in range(TERMS):
                    parts[i, t] = recv_e[it, d, t].astype(jnp.float32)
            sums = []
            for i, d in enumerate(slots):
                weighed = jnp.concatenate(
                    [
                        jnp.concatenate(
                            [
                                rowoh[d, q]
                                * jnp.broadcast_to(
                                    parts[i, t, q : q + 1, :], (ROWS, LANES)
                                ).astype(jnp.bfloat16)
                                for t in range(TERMS)
                            ],
                            axis=0,
                        )
                        for q in range(HALF)
                    ],
                    axis=1,
                )
                columns = jnp.concatenate([coloh[d, q] for q in range(HALF)], axis=1)
                product = lax.dot_general(
                    weighed, columns, (((1,), (1,)), ((), ())), preferred_element_type=jnp.float32
                )
                second = jnp.broadcast_to(recv_i[d][0:1, 0:1], product.shape) >= PIX
                sums.append((jnp.where(second, 0.0, product), jnp.where(second, product, 0.0)))
            for t in range(TILE_DEV):
                total = sums[0][t]
                for part in sums[1:]:
                    total = total + part[t]
                acc[t] += total
            return carry

        lax.fori_loop(0, groups // TOGETHER, collect, 0)
        for t in range(TILE_DEV):
            change = (acc[t, 0:ROWS, :] + acc[t, ROWS : 2 * ROWS, :]) / jnp.maximum(
                acc[t, 2 * ROWS : 3 * ROWS, :], 1.0
            )
            for half in range(2):
                rows = pl.ds(SIDE * t + half, ROWS, stride=2)
                current[rows, :] = current[rows, :] + change[:, LANES * half : LANES * (half + 1)]
        if it + 1 < ITERS:
            table[...] = current[...].astype(jnp.bfloat16).astype(jnp.float32)

    sky_out[...] = current[...]
    lane = lax.broadcasted_iota(jnp.int32, (8, LANES), 1)
    fit = jnp.zeros((8, LANES), jnp.float32)
    for n in range(BASELINE_COUNT):
        fit = jnp.where(lane == n, baseline[n], fit)
    for l in range(DETECTORS_LOCAL):
        base_out[l] = fit[l : l + 1, 0:BASELINE_COUNT]

    wait_bytes(send_i, groups - 1, sent.at[0])
    for it in range(ITERS):
        base_sem = 1 + 5 * it
        wait_bytes(send_a.at[it], groups - 1, sent.at[base_sem])
        wait_bytes(send_b.at[it], groups - 1, sent.at[base_sem + 1])
        wait_bytes(send_c.at[it], groups - 1, sent.at[base_sem + 2])
        wait_bytes(recv_d.at[it], blocks - 1, sent.at[base_sem + 3])
        wait_bytes(send_e.at[it], groups - 1, sent.at[base_sem + 4])


def local(detector_samples, pixels, crossings, lengths, mode_templates, mixing, sky_map):
    groups = lax.axis_size("det")
    blocks = lax.axis_size("tile")
    chunks = SAMP_DEV // LANES
    vmem = pl.BlockSpec(memory_space=pltpu.VMEM)
    smem = pl.BlockSpec(memory_space=pltpu.SMEM)
    hbm = pl.BlockSpec(memory_space=pl.ANY)
    f32, bf16, i32 = jnp.float32, jnp.bfloat16, jnp.int32
    dma = pltpu.SemaphoreType.DMA
    sky, fit = pl.pallas_call(
        functools.partial(kernel, groups, blocks),
        out_shape=(
            jax.ShapeDtypeStruct((TILE_DEV * SIDE, SIDE), f32),
            jax.ShapeDtypeStruct((DETECTORS_LOCAL, 1, BASELINE_COUNT), f32),
        ),
        in_specs=[smem, smem] + [hbm] * 5,
        out_specs=(vmem, vmem),
        scratch_shapes=[
            pltpu.VMEM((DETECTORS_LOCAL, SAMP_DEV), f32),
            pltpu.VMEM((DETECTORS_LOCAL, SAMP_DEV), i32),
            pltpu.VMEM((DETECTORS_LOCAL * groups, MODES), f32),
            pltpu.VMEM((MODES, MODES), f32),
            pltpu.VMEM((TILE_DEV * SIDE, SIDE), f32),
            pltpu.SMEM((groups,), i32),
            pltpu.VMEM((8 * groups, MODES), f32),
            pltpu.VMEM((8 * chunks, LANES), i32),
            pltpu.VMEM((8 * chunks, LANES), f32),
            pltpu.VMEM((8 * chunks, LANES), i32),
            pltpu.VMEM((ENTRIES, HALF, LANES), i32),
            pltpu.VMEM((ENTRIES, TERMS, HALF, LANES), bf16),
            pltpu.VMEM((8 * chunks, LANES), f32),
            pltpu.VMEM((8 * chunks, LANES), f32),
            pltpu.VMEM((8 * groups, LANES), f32),
            pltpu.VMEM((8 * groups, 8 * groups), f32),
            pltpu.VMEM((TILE_DEV * SIDE, SIDE), f32),
            pltpu.VMEM((TOGETHER, SIDE, SIDE), f32),
            pltpu.VMEM((TOGETHER, TERMS, HALF, LANES), f32),
            pltpu.VMEM((TILE_DEV, TERMS * ROWS, COLS), f32),
            pltpu.VMEM((groups, HALF, COLS, LANES), bf16),
            pltpu.VMEM((groups, HALF, ROWS, LANES), bf16),
            pltpu.VMEM((groups, HALF, LANES), i32),
            pltpu.VMEM((groups, HALF, LANES), i32),
            pltpu.VMEM((ITERS, groups, HALF, LANES), bf16),
            pltpu.VMEM((ITERS, groups, HALF, LANES), bf16),
            pltpu.VMEM((ITERS, chunks, DETECTORS_LOCAL, LANES), f32),
            pltpu.VMEM((ITERS, groups, DETECTORS_LOCAL, LANES), f32),
            pltpu.VMEM((ITERS, groups, DETECTORS_LOCAL, LANES), f32),
            pltpu.VMEM((ITERS, chunks, DETECTORS_LOCAL, LANES), f32),
            pltpu.VMEM((ITERS, 8, LANES), f32),
            pltpu.VMEM((ITERS, blocks, 8, LANES), f32),
            pltpu.VMEM((ITERS, groups, TERMS, HALF, LANES), bf16),
            pltpu.VMEM((ITERS, groups, TERMS, HALF, LANES), bf16),
            dma((5,)),
            dma((1 + 5 * ITERS,)),
            dma((groups,)),
            dma((ITERS,)),
            dma((ITERS,)),
            dma((ITERS,)),
            dma((ITERS,)),
            dma((ITERS, groups)),
        ],
        compiler_params=pltpu.CompilerParams(
            collective_id=0, has_side_effects=True, vmem_limit_bytes=60 * 1024 * 1024
        ),
    )(crossings, lengths, detector_samples, pixels, mode_templates, mixing,
      sky_map.reshape(TILE_DEV * SIDE, SIDE))
    return sky.reshape(TILE_DEV, SIDE, SIDE), fit


def solution(mesh):
    placed = (
        P("det", "tile"),
        P("det", "tile"),
        P("det", "tile", None),
        P("det", "tile", None),
        P(),
        P(),
        P(("det", "tile"), None, None),
    )
    return jax.shard_map(
        local,
        mesh=mesh,
        in_specs=placed,
        out_specs=(P(("det", "tile"), None, None), P("det", "tile", None)),
        check_vma=False,
    )
```

```python
import functools

import jax
import jax.numpy as jnp
from jax import lax
from jax.experimental import pallas as pl
from jax.experimental.pallas import tpu as pltpu
from jax.sharding import PartitionSpec as P

SIDE = 128
PIX = 16384
TILE_DEV = 2
MODES = 64
DETECTORS_LOCAL = 4
SAMP_DEV = 4096
SEG_PER = 4
BASELINE_COUNT = 16
ITERS = 2
PART = SAMP_DEV // SEG_PER
ENTRIES = DETECTORS_LOCAL * SEG_PER
LANES = 128
COLS = 256
ROWS = PIX // COLS
HALF = PART // LANES
TERMS = 3
TOGETHER = 4
VMEM_BYTES = 32 * 1024 * 1024

HUBER = 1.345
EPS = 1e-05
MESH = pl.DeviceIdType.MESH
ZRING = 8


def kernel(
    groups,
    blocks,
    cross_hbm,
    len_hbm,
    det_hbm,
    pix_hbm,
    templ_hbm,
    mixing_hbm,
    sky_hbm,
    sky_out,
    base_out,
    cross_ref,
    len_ref,
    det_ref,
    pix_ref,
    templ_ref,
    mixing_ref,
    current,
    ent_ref,
    templ_h,
    code_h,
    det_h,
    seg_h,
    code_e,
    val_e,
    work,
    clean_h,
    stack,
    matrix,
    table,
    chosen,
    parts,
    acc,
    columns,
    coloh,
    rowoh,
    send_i,
    recv_i,
    send_a,
    recv_a,
    send_b,
    recv_b,
    send_c,
    recv_c,
    send_d,
    recv_d,
    send_e,
    recv_e,
    load_sem,
    sent,
    sem_i,
    sem_a,
    sem_b,
    sem_c,
    sem_d,
    sem_e,
):
    me = lax.axis_index("det")
    block = lax.axis_index("tile")
    chunks = SAMP_DEV // LANES
    xring = groups // ZRING
    my_x, my_z = lax.div(me, ZRING), lax.rem(me, ZRING)

    loads = [
        pltpu.make_async_copy(src, dst, load_sem.at[i])
        for i, (src, dst) in enumerate(
            ((cross_hbm, cross_ref), (pix_hbm, pix_ref), (len_hbm, len_ref), (det_hbm, det_ref),
             (templ_hbm, templ_ref), (mixing_hbm, mixing_ref), (sky_hbm, current))
        )
    ]
    for load in loads:
        load.start()

    def hops(dx, dz):
        return min(dx, xring - dx) + min(dz, ZRING - dz)

    xs = [lax.rem(my_x + dx, xring) * ZRING for dx in range(xring)]
    zs = [lax.rem(my_z + dz, ZRING) for dz in range(ZRING)]
    offsets = sorted(
        ((dx, dz) for dx in range(xring) for dz in range(ZRING) if dx or dz), key=lambda o: hops(*o)
    )
    near = [xs[dx] + zs[dz] for dx, dz in offsets]
    far = near[::-1]

    def copy_to(src, dst, send_sem, recv_sem, **place):
        return pltpu.make_async_remote_copy(
            src_ref=src, dst_ref=dst, send_sem=send_sem, recv_sem=recv_sem,
            device_id=place, device_id_type=MESH,
        )

    def wait_bytes(ref, count, sem):
        view = ref.at[pl.ds(0, count)]
        pltpu.make_async_copy(view, view, sem).wait()

    barrier = pltpu.get_barrier_semaphore()
    for o in far:
        pl.semaphore_signal(barrier, inc=1, device_id={"det": o}, device_id_type=MESH)
    others = [lax.rem(block + step, blocks) for step in range(1, blocks)]
    for b in others:
        pl.semaphore_signal(barrier, inc=1, device_id={"tile": b}, device_id_type=MESH)

    loads[0].wait()
    def entry_place(e):
        return e // SEG_PER, e % SEG_PER

    tiles = [cross_ref[entry_place(e)[0], 0, entry_place(e)[1]] for e in range(ENTRIES)]
    owners = [lax.div(tile, TILE_DEV * blocks) for tile in tiles]

    def find_entry(o, carry):
        found = jnp.int32(-1)
        for e in range(ENTRIES):
            found = jnp.where(owners[e] == o, e, found)
        ent_ref[o] = found
        return carry

    lax.fori_loop(0, groups, find_entry, 0)

    det_h[...] = jnp.zeros_like(det_h)
    code_h[...] = jnp.zeros_like(code_h)
    clean_h[...] = jnp.zeros_like(clean_h)
    stack[...] = jnp.zeros_like(stack)
    templ_h[...] = jnp.zeros_like(templ_h)
    loads[1].wait()
    for j in range(chunks):
        code_h[8 * j : 8 * j + DETECTORS_LOCAL, :] = pix_ref[:, LANES * j : LANES * (j + 1)]

    def entry_rows(e):
        l, k = entry_place(e)
        return pl.ds(8 * HALF * k + l, HALF, stride=8)

    for e in range(ENTRIES):
        code_e[e] = code_h[entry_rows(e), :] + lax.rem(tiles[e], TILE_DEV) * PIX

    def pack_codes(o, carry):
        e = ent_ref[o]
        rows = code_e[jnp.maximum(e, 0)]
        send_i[o] = jnp.where(jnp.full(rows.shape, e, jnp.int32) >= 0, rows, -1)
        return carry

    lax.fori_loop(0, groups, pack_codes, 0)
    recv_i[me] = send_i[me]
    for load in loads[2:]:
        load.wait()

    pl.semaphore_wait(barrier, groups - 1 + blocks - 1)
    for o in near:
        copy_to(send_i.at[o], recv_i.at[me], sent.at[0], sem_i.at[me], det=o).start()

    for j in range(chunks):
        det_h[8 * j : 8 * j + DETECTORS_LOCAL, :] = det_ref[:, LANES * j : LANES * (j + 1)]
    table[...] = current[...].astype(jnp.bfloat16).astype(jnp.float32)
    templates = templ_ref[...].T
    for d in range(groups):
        templ_h[8 * d : 8 * d + DETECTORS_LOCAL, :] = templates[
            DETECTORS_LOCAL * d : DETECTORS_LOCAL * (d + 1), :
        ]
    mixed = jnp.dot(
        templ_h[...], mixing_ref[...],
        precision=lax.Precision.HIGHEST, preferred_element_type=jnp.float32,
    )
    matrix[...] = lax.dot_general(
        mixed, templ_h[...], (((1,), (1,)), ((), ())),
        precision=lax.Precision.HIGHEST, preferred_element_type=jnp.float32,
    )
    home = (chunks, 8, LANES)
    position = (
        lax.broadcasted_iota(jnp.int32, home, 0) * LANES + lax.broadcasted_iota(jnp.int32, home, 2)
    )
    sublane = lax.broadcasted_iota(jnp.int32, (8, LANES), 0)
    ends = [jnp.int32(0)] * DETECTORS_LOCAL
    seg = jnp.zeros(home, jnp.int32)
    for n in range(BASELINE_COUNT):
        end = jnp.zeros((8, LANES), jnp.int32)
        for l in range(DETECTORS_LOCAL):
            ends[l] = ends[l] + len_ref[l, 0, n]
            end = jnp.where(sublane == l, ends[l], end)
        seg += (position >= end[None]).astype(jnp.int32)
    seg_h[...] = seg.reshape(8 * chunks, LANES)

    def turn_columns():
        column = jnp.bitwise_and(recv_i[...].reshape(groups * HALF, LANES), COLS - 1).T
        for part in range(groups * HALF // LANES):
            columns[part] = column[:, LANES * part : LANES * (part + 1)]

    def flags(part):
        slots = LANES // HALF

        def one(i, carry):
            d = slots * part + i
            code = recv_i[d]
            row = jnp.where(
                code < 0, -1, jnp.bitwise_and(lax.shift_right_arithmetic(code, 8), ROWS - 1)
            )
            square = (LANES, LANES)
            lane = lax.broadcasted_iota(jnp.int32, square, 1)
            for q in range(HALF):
                rowoh[d, q] = (
                    jnp.broadcast_to(row[q : q + 1, :], (ROWS, LANES))
                    == lax.broadcasted_iota(jnp.int32, (ROWS, LANES), 0)
                ).astype(jnp.float32).astype(jnp.bfloat16)
                col = jnp.take_along_axis(
                    columns[part], jnp.full(square, HALF * i + q, jnp.int32), axis=1
                )
                for h in range(COLS // LANES):
                    coloh[d, h, LANES * q : LANES * (q + 1), :] = (
                        col == lane + LANES * h
                    ).astype(jnp.float32).astype(jnp.bfloat16)
            return carry

        lax.fori_loop(0, slots, one, 0)

    def peer_of(step):
        x = lax.rem(my_x + lax.div(step, ZRING), xring)
        z = lax.rem(my_z + lax.rem(step, ZRING), ZRING)
        return x * ZRING + z

    baseline = [jnp.zeros((8, 1), jnp.float32) for _ in range(BASELINE_COUNT)]

    for it in range(ITERS):
        base_sem = 1 + 5 * it

        def answer(batch, carry):
            slots = [
                peer_of(step if it == 0 else lax.rem(step + 20, groups))
                for step in (TOGETHER * batch + i for i in range(TOGETHER))
            ]
            if it == 0:
                for i, d in enumerate(slots):
                    @pl.when(TOGETHER * batch + i > 0)
                    def _():
                        copy_to(
                            send_i.at[d], recv_i.at[d], sent.at[0], sem_i.at[d], det=d
                        ).wait_recv()
            values = []
            for i, d in enumerate(slots):
                code = recv_i[d]
                row = jnp.bitwise_and(lax.shift_right_arithmetic(code, 7), SIDE - 1)
                col = jnp.bitwise_and(code, LANES - 1)
                second = code >= PIX
                for g in range(SIDE // 8):
                    chosen[i, 8 * g : 8 * g + 8, :] = jnp.where(
                        second,
                        table[SIDE + 8 * g : SIDE + 8 * g + 8, :],
                        table[8 * g : 8 * g + 8, :],
                    )
                value = jnp.zeros((HALF, LANES), jnp.float32)
                for r in range(SIDE):
                    line = jnp.broadcast_to(chosen[i, r : r + 1, :], (HALF, LANES))
                    value = jnp.where(row == r, jnp.take_along_axis(line, col, axis=1), value)
                values.append(value)
            for d, value in zip(slots, values):
                send_a[it, d] = value.astype(jnp.bfloat16)
            for d in slots:
                @pl.when(d != me)
                def _():
                    copy_to(
                        send_a.at[it, d], recv_a.at[it, me], sent.at[base_sem], sem_a.at[it], det=d
                    ).start()

            return carry

        lax.fori_loop(0, groups // TOGETHER, answer, 0)
        recv_a[it, me] = send_a[it, me]
        if it == 0:
            turn_columns()
            flags(0)
        wait_bytes(recv_a.at[it], groups - 1, sem_a.at[it])

        for e in range(ENTRIES):
            work[entry_rows(e), :] = recv_a[it, owners[e]].astype(jnp.float32)
        residual = det_h[...] - work[...]
        for j in range(chunks):
            send_b[it, j] = residual[8 * j : 8 * j + DETECTORS_LOCAL, :]
        recv_b[it, me] = send_b[it, me]
        for j in far:
            copy_to(
                send_b.at[it, j], recv_b.at[it, me], sent.at[base_sem + 1], sem_b.at[it], det=j
            ).start()
        if it == 0:
            flags(1)
        wait_bytes(recv_b.at[it], groups - 1, sem_b.at[it])

        for d in range(groups):
            stack[8 * d : 8 * d + DETECTORS_LOCAL, :] = recv_b[it, d]
        every = stack[...]
        every = every - jnp.dot(
            matrix[...], every,
            precision=lax.Precision.HIGHEST, preferred_element_type=jnp.float32,
        )
        for d in range(groups):
            send_c[it, d] = every[8 * d : 8 * d + DETECTORS_LOCAL, :]
        recv_c[it, me] = send_c[it, me]
        for d in far:
            copy_to(
                send_c.at[it, d], recv_c.at[it, me], sent.at[base_sem + 2], sem_c.at[it], det=d
            ).start()
        acc[...] = jnp.zeros_like(acc)
        wait_bytes(recv_c.at[it], groups - 1, sem_c.at[it])

        for j in range(chunks):
            clean_h[8 * j : 8 * j + DETECTORS_LOCAL, :] = recv_c[it, j]
        cleaned = clean_h[...].reshape(home)
        send_d[it] = jnp.sum(cleaned * cleaned, axis=0)
        recv_d[it, block] = send_d[it]
        for b in others:
            copy_to(
                send_d.at[it], recv_d.at[it, block], sent.at[base_sem + 3], sem_d.at[it], tile=b
            ).start()
        wait_bytes(recv_d.at[it], blocks - 1, sem_d.at[it])
        squares = jnp.sum(jnp.sum(recv_d[it], axis=0), axis=1, keepdims=True)
        level = HUBER * jnp.sqrt(squares / (SAMP_DEV * blocks) + EPS)
        weight = level[None] / jnp.maximum(jnp.abs(cleaned), level[None])
        weighted = weight * cleaned
        seg = seg_h[...].reshape(home)
        stepped = jnp.zeros(home, jnp.float32)
        for n in range(BASELINE_COUNT):
            inside = seg == n
            numerator = jnp.sum(
                jnp.sum(jnp.where(inside, weighted, 0.0), axis=0), axis=1, keepdims=True
            )
            denominator = jnp.sum(
                jnp.sum(jnp.where(inside, weight, 0.0), axis=0), axis=1, keepdims=True
            )
            increment = numerator / jnp.where(denominator > 0.0, denominator, 1.0)
            baseline[n] = baseline[n] + increment
            stepped = jnp.where(inside, increment[None], stepped)
        if it + 1 < ITERS:
            det_h[...] = det_h[...] - stepped.reshape(8 * chunks, LANES)
        work[...] = (weight * (cleaned - stepped)).reshape(8 * chunks, LANES)
        clean_h[...] = weight.reshape(8 * chunks, LANES)
        for e in range(ENTRIES):
            value = work[entry_rows(e), :]
            high = value.astype(jnp.bfloat16)
            val_e[e, 0] = high
            val_e[e, 1] = (value - high.astype(jnp.float32)).astype(jnp.bfloat16)
            val_e[e, 2] = clean_h[entry_rows(e), :].astype(jnp.bfloat16)

        for o in near:
            send_e[it, o] = val_e[jnp.maximum(ent_ref[o], 0)]
            copy_to(
                send_e.at[it, o], recv_e.at[it, me], sent.at[base_sem + 4], sem_e.at[it, me], det=o
            ).start()
        recv_e[it, me] = val_e[jnp.maximum(ent_ref[me], 0)]
        clean_h[...] = jnp.zeros_like(clean_h)

        def collect(batch, carry):
            slots = [peer_of(TOGETHER * batch + i) for i in range(TOGETHER)]
            for i, d in enumerate(slots):
                @pl.when(TOGETHER * batch + i > 0)
                def _():
                    copy_to(
                        send_e.at[it, d], recv_e.at[it, d], sent.at[base_sem + 4], sem_e.at[it, d],
                        det=d,
                    ).wait_recv()
            for i, d in enumerate(slots):
                for t in range(TERMS):
                    parts[i, t] = recv_e[it, d, t].astype(jnp.float32)
            sums = []
            for i, d in enumerate(slots):
                weighed = jnp.concatenate(
                    [
                        jnp.concatenate(
                            [
                                rowoh[d, q]
                                * jnp.broadcast_to(
                                    parts[i, t, q : q + 1, :], (ROWS, LANES)
                                ).astype(jnp.bfloat16)
                                for t in range(TERMS)
                            ],
                            axis=0,
                        )
                        for q in range(HALF)
                    ],
                    axis=1,
                )
                spread = jnp.concatenate([coloh[d, h] for h in range(COLS // LANES)], axis=1)
                product = jnp.dot(weighed, spread, preferred_element_type=jnp.float32)
                second = jnp.broadcast_to(recv_i[d][0:1, 0:1], product.shape) >= PIX
                sums.append((jnp.where(second, 0.0, product), jnp.where(second, product, 0.0)))
            for t in range(TILE_DEV):
                total = sums[0][t]
                for part in sums[1:]:
                    total = total + part[t]
                acc[t] += total
            return carry

        lax.fori_loop(0, groups // TOGETHER, collect, 0)
        for t in range(TILE_DEV):
            change = (acc[t, 0:ROWS, :] + acc[t, ROWS : 2 * ROWS, :]) / jnp.maximum(
                acc[t, 2 * ROWS : 3 * ROWS, :], 1.0
            )
            for half in range(2):
                rows = pl.ds(SIDE * t + half, ROWS, stride=2)
                current[rows, :] = current[rows, :] + change[:, LANES * half : LANES * (half + 1)]
        if it + 1 < ITERS:
            table[...] = current[...].astype(jnp.bfloat16).astype(jnp.float32)

    sky_out[...] = current[...]
    lane = lax.broadcasted_iota(jnp.int32, (8, LANES), 1)
    fit = jnp.zeros((8, LANES), jnp.float32)
    for n in range(BASELINE_COUNT):
        fit = jnp.where(lane == n, baseline[n], fit)
    for l in range(DETECTORS_LOCAL):
        base_out[l] = fit[l : l + 1, 0:BASELINE_COUNT]

    wait_bytes(send_i, groups - 1, sent.at[0])
    for it in range(ITERS):
        base_sem = 1 + 5 * it
        wait_bytes(send_a.at[it], groups - 1, sent.at[base_sem])
        wait_bytes(send_b.at[it], groups - 1, sent.at[base_sem + 1])
        wait_bytes(send_c.at[it], groups - 1, sent.at[base_sem + 2])
        wait_bytes(recv_d.at[it], blocks - 1, sent.at[base_sem + 3])
        wait_bytes(send_e.at[it], groups - 1, sent.at[base_sem + 4])


def local(detector_samples, pixels, crossings, lengths, mode_templates, mixing, sky_map):
    groups = lax.axis_size("det")
    blocks = lax.axis_size("tile")
    chunks = SAMP_DEV // LANES
    vmem = pl.BlockSpec(memory_space=pltpu.VMEM)
    hbm = pl.BlockSpec(memory_space=pltpu.HBM)
    f32, bf16, i32 = jnp.float32, jnp.bfloat16, jnp.int32
    dma = pltpu.SemaphoreType.DMA
    sky, fit = pl.pallas_call(
        functools.partial(kernel, groups, blocks),
        out_shape=(
            jax.ShapeDtypeStruct((TILE_DEV * SIDE, SIDE), f32),
            jax.ShapeDtypeStruct((DETECTORS_LOCAL, 1, BASELINE_COUNT), f32),
        ),
        in_specs=[hbm] * 7,
        out_specs=(vmem, vmem),
        scratch_shapes=[
            pltpu.SMEM((DETECTORS_LOCAL, 1, SEG_PER), i32),
            pltpu.SMEM((DETECTORS_LOCAL, 1, BASELINE_COUNT), i32),
            pltpu.VMEM((DETECTORS_LOCAL, SAMP_DEV), f32),
            pltpu.VMEM((DETECTORS_LOCAL, SAMP_DEV), i32),
            pltpu.VMEM((MODES, DETECTORS_LOCAL * groups), f32),
            pltpu.VMEM((MODES, MODES), f32),
            pltpu.VMEM((TILE_DEV * SIDE, SIDE), f32),
            pltpu.SMEM((groups,), i32),
            pltpu.VMEM((8 * groups, MODES), f32),
            pltpu.VMEM((8 * chunks, LANES), i32),
            pltpu.VMEM((8 * chunks, LANES), f32),
            pltpu.VMEM((8 * chunks, LANES), i32),
            pltpu.VMEM((ENTRIES, HALF, LANES), i32),
            pltpu.VMEM((ENTRIES, TERMS, HALF, LANES), bf16),
            pltpu.VMEM((8 * chunks, LANES), f32),
            pltpu.VMEM((8 * chunks, LANES), f32),
            pltpu.VMEM((8 * groups, LANES), f32),
            pltpu.VMEM((8 * groups, 8 * groups), f32),
            pltpu.VMEM((TILE_DEV * SIDE, SIDE), f32),
            pltpu.VMEM((TOGETHER, SIDE, SIDE), f32),
            pltpu.VMEM((TOGETHER, TERMS, HALF, LANES), f32),
            pltpu.VMEM((TILE_DEV, TERMS * ROWS, COLS), f32),
            pltpu.VMEM((groups * HALF // LANES, LANES, LANES), i32),
            pltpu.VMEM((groups, COLS // LANES, PART, LANES), bf16),
            pltpu.VMEM((groups, HALF, ROWS, LANES), bf16),
            pltpu.VMEM((groups, HALF, LANES), i32),
            pltpu.VMEM((groups, HALF, LANES), i32),
            pltpu.VMEM((ITERS, groups, HALF, LANES), bf16),
            pltpu.VMEM((ITERS, groups, HALF, LANES), bf16),
            pltpu.VMEM((ITERS, chunks, DETECTORS_LOCAL, LANES), f32),
            pltpu.VMEM((ITERS, groups, DETECTORS_LOCAL, LANES), f32),
            pltpu.VMEM((ITERS, groups, DETECTORS_LOCAL, LANES), f32),
            pltpu.VMEM((ITERS, chunks, DETECTORS_LOCAL, LANES), f32),
            pltpu.VMEM((ITERS, 8, LANES), f32),
            pltpu.VMEM((ITERS, blocks, 8, LANES), f32),
            pltpu.VMEM((ITERS, groups, TERMS, HALF, LANES), bf16),
            pltpu.VMEM((ITERS, groups, TERMS, HALF, LANES), bf16),
            dma((7,)),
            dma((1 + 5 * ITERS,)),
            dma((groups,)),
            dma((ITERS,)),
            dma((ITERS,)),
            dma((ITERS,)),
            dma((ITERS,)),
            dma((ITERS, groups)),
        ],
        compiler_params=pltpu.CompilerParams(
            collective_id=0, has_side_effects=True, vmem_limit_bytes=VMEM_BYTES
        ),
    )(*(
        pltpu.with_memory_space_constraint(array, pltpu.HBM)
        for array in (
            crossings, lengths, detector_samples, pixels, mode_templates.T, mixing,
            sky_map.reshape(TILE_DEV * SIDE, SIDE),
        )
    ))
    return sky.reshape(TILE_DEV, SIDE, SIDE), fit


def solution(mesh):
    placed = (
        P("det", "tile"),
        P("det", "tile"),
        P("det", "tile", None),
        P("det", "tile", None),
        P(),
        P(),
        P(("det", "tile"), None, None),
    )
    return jax.shard_map(
        local,
        mesh=mesh,
        in_specs=placed,
        out_specs=(P(("det", "tile"), None, None), P("det", "tile", None)),
        check_vma=False,
    )
```

```python
import functools

import jax
import jax.numpy as jnp
from jax import lax
from jax.experimental import pallas as pl
from jax.experimental.pallas import tpu as pltpu
from jax.sharding import PartitionSpec as P

SIDE = 128
PIX = 16384
TILE_DEV = 2
MODES = 64
DETECTORS_LOCAL = 4
SAMP_DEV = 4096
SEG_PER = 4
BASELINE_COUNT = 16
ITERS = 2
PART = SAMP_DEV // SEG_PER
ENTRIES = DETECTORS_LOCAL * SEG_PER
LANES = 128
COLS = 256
ROWS = PIX // COLS
HALF = PART // LANES
TERMS = 3
SEG_BITS = 16
SEG_UNIT = 1 << SEG_BITS
TOGETHER = 4
VMEM_BYTES = 32 * 1024 * 1024

HUBER = 1.345
EPS = 1e-05
MESH = pl.DeviceIdType.MESH
ZRING = 8


def kernel(
    groups,
    blocks,
    cross_hbm,
    len_hbm,
    det_hbm,
    pix_hbm,
    templ_hbm,
    mixing_hbm,
    sky_hbm,
    sky_out,
    base_out,
    cross_ref,
    len_ref,
    det_ref,
    pix_ref,
    templ_ref,
    mixing_ref,
    current,
    ent_ref,
    templ_h,
    code_h,
    det_h,
    seg_h,
    code_e,
    val_e,
    work,
    clean_h,
    stack,
    matrix,
    table,
    chosen,
    parts,
    acc,
    columns,
    coloh,
    rowoh,
    send_i,
    recv_i,
    send_a,
    recv_a,
    send_b,
    recv_b,
    send_c,
    recv_c,
    send_d,
    recv_d,
    send_e,
    recv_e,
    head,
    send_h,
    recv_h,
    load_sem,
    sent,
    sem_i,
    sem_a,
    sem_b,
    sem_c,
    sem_d,
    sem_e,
    sem_h,
):
    me = lax.axis_index("det")
    block = lax.axis_index("tile")
    chunks = SAMP_DEV // LANES
    xring = groups // ZRING
    my_x, my_z = lax.div(me, ZRING), lax.rem(me, ZRING)

    loads = [
        pltpu.make_async_copy(src, dst, load_sem.at[i])
        for i, (src, dst) in enumerate(
            ((cross_hbm, cross_ref), (pix_hbm, pix_ref), (len_hbm, len_ref), (det_hbm, det_ref),
             (templ_hbm, templ_ref), (mixing_hbm, mixing_ref), (sky_hbm, current))
        )
    ]
    for load in loads:
        load.start()

    def hops(dx, dz):
        return min(dx, xring - dx) + min(dz, ZRING - dz)

    xs = [lax.rem(my_x + dx, xring) * ZRING for dx in range(xring)]
    zs = [lax.rem(my_z + dz, ZRING) for dz in range(ZRING)]
    offsets = sorted(
        ((dx, dz) for dx in range(xring) for dz in range(ZRING) if dx or dz), key=lambda o: hops(*o)
    )
    near = [xs[dx] + zs[dz] for dx, dz in offsets]
    far = near[::-1]

    def copy_to(src, dst, send_sem, recv_sem, **place):
        return pltpu.make_async_remote_copy(
            src_ref=src, dst_ref=dst, send_sem=send_sem, recv_sem=recv_sem,
            device_id=place, device_id_type=MESH,
        )

    def wait_bytes(ref, count, sem):
        view = ref.at[pl.ds(0, count)]
        pltpu.make_async_copy(view, view, sem).wait()

    barrier = pltpu.get_barrier_semaphore()
    for o in far:
        pl.semaphore_signal(barrier, inc=1, device_id={"det": o}, device_id_type=MESH)
    others = [lax.rem(block + step, blocks) for step in range(1, blocks)]
    for b in others:
        pl.semaphore_signal(barrier, inc=1, device_id={"tile": b}, device_id_type=MESH)

    loads[0].wait()
    def entry_place(e):
        return e // SEG_PER, e % SEG_PER

    tiles = [cross_ref[entry_place(e)[0], 0, entry_place(e)[1]] for e in range(ENTRIES)]
    owners = [lax.div(tile, TILE_DEV * blocks) for tile in tiles]

    def find_entry(o, carry):
        found = jnp.int32(-1)
        for e in range(ENTRIES):
            found = jnp.where(owners[e] == o, e, found)
        ent_ref[o] = found
        return carry

    lax.fori_loop(0, groups, find_entry, 0)

    det_h[...] = jnp.zeros_like(det_h)
    code_h[...] = jnp.zeros_like(code_h)
    clean_h[...] = jnp.zeros_like(clean_h)
    stack[...] = jnp.zeros_like(stack)
    templ_h[...] = jnp.zeros_like(templ_h)
    loads[1].wait()
    for j in range(chunks):
        code_h[8 * j : 8 * j + DETECTORS_LOCAL, :] = pix_ref[:, LANES * j : LANES * (j + 1)]

    loads[2].wait()
    home = (chunks, 8, LANES)
    position = (
        lax.broadcasted_iota(jnp.int32, home, 0) * LANES + lax.broadcasted_iota(jnp.int32, home, 2)
    )
    sublane = lax.broadcasted_iota(jnp.int32, (8, LANES), 0)
    ends = [jnp.int32(0)] * DETECTORS_LOCAL
    seg = jnp.zeros(home, jnp.int32)
    for n in range(BASELINE_COUNT):
        end = jnp.zeros((8, LANES), jnp.int32)
        for l in range(DETECTORS_LOCAL):
            ends[l] = ends[l] + len_ref[l, 0, n]
            end = jnp.where(sublane == l, ends[l], end)
        seg += (position >= end[None]).astype(jnp.int32)
    seg_h[...] = seg.reshape(8 * chunks, LANES)

    def entry_rows(e):
        l, k = entry_place(e)
        return pl.ds(8 * HALF * k + l, HALF, stride=8)

    for e in range(ENTRIES):
        code_e[e] = (
            code_h[entry_rows(e), :]
            + lax.rem(tiles[e], TILE_DEV) * PIX
            + seg_h[entry_rows(e), :] * SEG_UNIT
        )

    def pack_codes(o, carry):
        e = ent_ref[o]
        rows = code_e[jnp.maximum(e, 0)]
        send_i[o] = jnp.where(jnp.full(rows.shape, e, jnp.int32) >= 0, rows, -1)
        return carry

    lax.fori_loop(0, groups, pack_codes, 0)
    recv_i[me] = send_i[me]
    for load in loads[3:]:
        load.wait()

    pl.semaphore_wait(barrier, groups - 1 + blocks - 1)
    for o in near:
        copy_to(send_i.at[o], recv_i.at[me], sent.at[0], sem_i.at[me], det=o).start()

    for j in range(chunks):
        det_h[8 * j : 8 * j + DETECTORS_LOCAL, :] = det_ref[:, LANES * j : LANES * (j + 1)]
    table[...] = current[...].astype(jnp.bfloat16).astype(jnp.float32)
    templates = templ_ref[...].T
    for d in range(groups):
        templ_h[8 * d : 8 * d + DETECTORS_LOCAL, :] = templates[
            DETECTORS_LOCAL * d : DETECTORS_LOCAL * (d + 1), :
        ]
    mixed = jnp.dot(
        templ_h[...], mixing_ref[...],
        precision=lax.Precision.HIGHEST, preferred_element_type=jnp.float32,
    )
    matrix[...] = lax.dot_general(
        mixed, templ_h[...], (((1,), (1,)), ((), ())),
        precision=lax.Precision.HIGHEST, preferred_element_type=jnp.float32,
    )
    def turn_columns():
        column = jnp.bitwise_and(recv_i[...].reshape(groups * HALF, LANES), COLS - 1).T
        for part in range(groups * HALF // LANES):
            columns[part] = column[:, LANES * part : LANES * (part + 1)]

    def flags(part):
        slots = LANES // HALF

        def one(i, carry):
            d = slots * part + i
            code = recv_i[d]
            row = jnp.where(
                code < 0, -1, jnp.bitwise_and(lax.shift_right_arithmetic(code, 8), ROWS - 1)
            )
            square = (LANES, LANES)
            lane = lax.broadcasted_iota(jnp.int32, square, 1)
            for q in range(HALF):
                rowoh[d, q] = (
                    jnp.broadcast_to(row[q : q + 1, :], (ROWS, LANES))
                    == lax.broadcasted_iota(jnp.int32, (ROWS, LANES), 0)
                ).astype(jnp.float32).astype(jnp.bfloat16)
                col = jnp.take_along_axis(
                    columns[part], jnp.full(square, HALF * i + q, jnp.int32), axis=1
                )
                for h in range(COLS // LANES):
                    coloh[d, h, LANES * q : LANES * (q + 1), :] = (
                        col == lane + LANES * h
                    ).astype(jnp.float32).astype(jnp.bfloat16)
            return carry

        lax.fori_loop(0, slots, one, 0)

    def peer_of(step):
        x = lax.rem(my_x + lax.div(step, ZRING), xring)
        z = lax.rem(my_z + lax.rem(step, ZRING), ZRING)
        return x * ZRING + z

    baseline = [jnp.zeros((8, 1), jnp.float32) for _ in range(BASELINE_COUNT)]

    for it in range(ITERS):
        base_sem = 1 + 6 * it

        def answer(batch, carry):
            slots = [
                peer_of(step if it == 0 else lax.rem(step + 20, groups))
                for step in (TOGETHER * batch + i for i in range(TOGETHER))
            ]
            if it == 0:
                for i, d in enumerate(slots):
                    @pl.when(TOGETHER * batch + i > 0)
                    def _():
                        copy_to(
                            send_i.at[d], recv_i.at[d], sent.at[0], sem_i.at[d], det=d
                        ).wait_recv()
            values = []
            for i, d in enumerate(slots):
                code = recv_i[d]
                row = jnp.bitwise_and(lax.shift_right_arithmetic(code, 7), SIDE - 1)
                col = jnp.bitwise_and(code, LANES - 1)
                second = jnp.bitwise_and(code, PIX) > 0
                for g in range(SIDE // 8):
                    chosen[i, 8 * g : 8 * g + 8, :] = jnp.where(
                        second,
                        table[SIDE + 8 * g : SIDE + 8 * g + 8, :],
                        table[8 * g : 8 * g + 8, :],
                    )
                value = jnp.zeros((HALF, LANES), jnp.float32)
                for r in range(SIDE):
                    line = jnp.broadcast_to(chosen[i, r : r + 1, :], (HALF, LANES))
                    value = jnp.where(row == r, jnp.take_along_axis(line, col, axis=1), value)
                values.append(value)
            for d, value in zip(slots, values):
                send_a[it, d] = value.astype(jnp.bfloat16)
            for d in slots:
                @pl.when(d != me)
                def _():
                    copy_to(
                        send_a.at[it, d], recv_a.at[it, me], sent.at[base_sem], sem_a.at[it], det=d
                    ).start()

            return carry

        lax.fori_loop(0, groups // TOGETHER, answer, 0)
        recv_a[it, me] = send_a[it, me]
        if it == 0:
            turn_columns()
            flags(0)
        wait_bytes(recv_a.at[it], groups - 1, sem_a.at[it])

        for e in range(ENTRIES):
            work[entry_rows(e), :] = recv_a[it, owners[e]].astype(jnp.float32)
        residual = det_h[...] - work[...]
        for j in range(chunks):
            send_b[it, j] = residual[8 * j : 8 * j + DETECTORS_LOCAL, :]
        recv_b[it, me] = send_b[it, me]
        for j in far:
            copy_to(
                send_b.at[it, j], recv_b.at[it, me], sent.at[base_sem + 1], sem_b.at[it], det=j
            ).start()
        if it == 0:
            flags(1)
        wait_bytes(recv_b.at[it], groups - 1, sem_b.at[it])

        for d in range(groups):
            stack[8 * d : 8 * d + DETECTORS_LOCAL, :] = recv_b[it, d]
        every = stack[...]
        every = every - jnp.dot(
            matrix[...], every,
            precision=lax.Precision.HIGHEST, preferred_element_type=jnp.float32,
        )
        for d in range(groups):
            send_c[it, d] = every[8 * d : 8 * d + DETECTORS_LOCAL, :]
        recv_c[it, me] = send_c[it, me]
        for d in far:
            copy_to(
                send_c.at[it, d], recv_c.at[it, me], sent.at[base_sem + 2], sem_c.at[it], det=d
            ).start()
        acc[...] = jnp.zeros_like(acc)
        wait_bytes(recv_c.at[it], groups - 1, sem_c.at[it])

        for j in range(chunks):
            clean_h[8 * j : 8 * j + DETECTORS_LOCAL, :] = recv_c[it, j]
        cleaned = clean_h[...].reshape(home)
        send_d[it] = jnp.sum(cleaned * cleaned, axis=0)
        recv_d[it, block] = send_d[it]
        for b in others:
            copy_to(
                send_d.at[it], recv_d.at[it, block], sent.at[base_sem + 3], sem_d.at[it], tile=b
            ).start()
        for e in range(ENTRIES):
            val_e[e] = clean_h[entry_rows(e), :]
        for o in near:
            send_e[it, o] = val_e[jnp.maximum(ent_ref[o], 0)]
            copy_to(
                send_e.at[it, o], recv_e.at[it, me], sent.at[base_sem + 4], sem_e.at[it, me], det=o
            ).start()
        recv_e[it, me] = val_e[jnp.maximum(ent_ref[me], 0)]
        wait_bytes(recv_d.at[it], blocks - 1, sem_d.at[it])
        squares = jnp.sum(jnp.sum(recv_d[it], axis=0), axis=1, keepdims=True)
        level = HUBER * jnp.sqrt(squares / (SAMP_DEV * blocks) + EPS)
        weight = level[None] / jnp.maximum(jnp.abs(cleaned), level[None])
        weighted = weight * cleaned
        seg = seg_h[...].reshape(home)
        lane = lax.broadcasted_iota(jnp.int32, (8, LANES), 1)
        line = jnp.where(lane == BASELINE_COUNT, level, 0.0)
        increments = []
        for n in range(BASELINE_COUNT):
            inside = seg == n
            numerator = jnp.sum(
                jnp.sum(jnp.where(inside, weighted, 0.0), axis=0), axis=1, keepdims=True
            )
            denominator = jnp.sum(
                jnp.sum(jnp.where(inside, weight, 0.0), axis=0), axis=1, keepdims=True
            )
            increment = numerator / jnp.where(denominator > 0.0, denominator, 1.0)
            increments.append(increment)
            line = jnp.where(lane == n, increment, line)
        for l in range(DETECTORS_LOCAL):
            head[l] = line[l : l + 1, :]
        for o in near:
            send_h[it, o] = head[lax.div(jnp.maximum(ent_ref[o], 0), SEG_PER)]
            copy_to(
                send_h.at[it, o], recv_h.at[it, me], sent.at[base_sem + 5], sem_h.at[it, me], det=o
            ).start()
        recv_h[it, me] = head[lax.div(jnp.maximum(ent_ref[me], 0), SEG_PER)]
        for n in range(BASELINE_COUNT):
            baseline[n] = baseline[n] + increments[n]
        if it + 1 < ITERS:
            stepped = jnp.zeros(home, jnp.float32)
            for n in range(BASELINE_COUNT):
                stepped = jnp.where(seg == n, increments[n][None], stepped)
            det_h[...] = det_h[...] - stepped.reshape(8 * chunks, LANES)

        def collect(batch, carry):
            slots = [peer_of(TOGETHER * batch + i) for i in range(TOGETHER)]
            for i, d in enumerate(slots):
                @pl.when(TOGETHER * batch + i > 0)
                def _():
                    copy_to(
                        send_e.at[it, d], recv_e.at[it, d], sent.at[base_sem + 4], sem_e.at[it, d],
                        det=d,
                    ).wait_recv()
                    copy_to(
                        send_h.at[it, d], recv_h.at[it, d], sent.at[base_sem + 5], sem_h.at[it, d],
                        det=d,
                    ).wait_recv()
            for i, d in enumerate(slots):
                cleaned_d = recv_e[it, d]
                line = jnp.broadcast_to(recv_h[it, d], (HALF, LANES))
                seg_d = jnp.bitwise_and(
                    lax.shift_right_arithmetic(recv_i[d], SEG_BITS), BASELINE_COUNT - 1
                )
                step_d = jnp.take_along_axis(line, seg_d, axis=1)
                level_d = jnp.take_along_axis(
                    line, jnp.full((HALF, LANES), BASELINE_COUNT, jnp.int32), axis=1
                )
                weight_d = level_d / jnp.maximum(jnp.abs(cleaned_d), level_d)
                value_d = weight_d * (cleaned_d - step_d)
                high = value_d.astype(jnp.bfloat16).astype(jnp.float32)
                parts[i, 0] = high
                parts[i, 1] = value_d - high
                parts[i, 2] = weight_d
            sums = []
            for i, d in enumerate(slots):
                weighed = jnp.concatenate(
                    [
                        jnp.concatenate(
                            [
                                rowoh[d, q]
                                * jnp.broadcast_to(
                                    parts[i, t, q : q + 1, :], (ROWS, LANES)
                                ).astype(jnp.bfloat16)
                                for t in range(TERMS)
                            ],
                            axis=0,
                        )
                        for q in range(HALF)
                    ],
                    axis=1,
                )
                spread = jnp.concatenate([coloh[d, h] for h in range(COLS // LANES)], axis=1)
                product = jnp.dot(weighed, spread, preferred_element_type=jnp.float32)
                second = (
                    jnp.broadcast_to(jnp.bitwise_and(recv_i[d], PIX)[0:1, 0:1], product.shape) > 0
                )
                sums.append((jnp.where(second, 0.0, product), jnp.where(second, product, 0.0)))
            for t in range(TILE_DEV):
                total = sums[0][t]
                for part in sums[1:]:
                    total = total + part[t]
                acc[t] += total
            return carry

        lax.fori_loop(0, groups // TOGETHER, collect, 0)
        for t in range(TILE_DEV):
            change = (acc[t, 0:ROWS, :] + acc[t, ROWS : 2 * ROWS, :]) / jnp.maximum(
                acc[t, 2 * ROWS : 3 * ROWS, :], 1.0
            )
            for half in range(2):
                rows = pl.ds(SIDE * t + half, ROWS, stride=2)
                current[rows, :] = current[rows, :] + change[:, LANES * half : LANES * (half + 1)]
        if it + 1 < ITERS:
            table[...] = current[...].astype(jnp.bfloat16).astype(jnp.float32)

    sky_out[...] = current[...]
    lane = lax.broadcasted_iota(jnp.int32, (8, LANES), 1)
    fit = jnp.zeros((8, LANES), jnp.float32)
    for n in range(BASELINE_COUNT):
        fit = jnp.where(lane == n, baseline[n], fit)
    for l in range(DETECTORS_LOCAL):
        base_out[l] = fit[l : l + 1, 0:BASELINE_COUNT]

    wait_bytes(send_i, groups - 1, sent.at[0])
    for it in range(ITERS):
        base_sem = 1 + 6 * it
        wait_bytes(send_a.at[it], groups - 1, sent.at[base_sem])
        wait_bytes(send_b.at[it], groups - 1, sent.at[base_sem + 1])
        wait_bytes(send_c.at[it], groups - 1, sent.at[base_sem + 2])
        wait_bytes(recv_d.at[it], blocks - 1, sent.at[base_sem + 3])
        wait_bytes(send_e.at[it], groups - 1, sent.at[base_sem + 4])
        wait_bytes(send_h.at[it], groups - 1, sent.at[base_sem + 5])


def local(detector_samples, pixels, crossings, lengths, mode_templates, mixing, sky_map):
    groups = lax.axis_size("det")
    blocks = lax.axis_size("tile")
    chunks = SAMP_DEV // LANES
    vmem = pl.BlockSpec(memory_space=pltpu.VMEM)
    hbm = pl.BlockSpec(memory_space=pltpu.HBM)
    f32, bf16, i32 = jnp.float32, jnp.bfloat16, jnp.int32
    dma = pltpu.SemaphoreType.DMA
    sky, fit = pl.pallas_call(
        functools.partial(kernel, groups, blocks),
        out_shape=(
            jax.ShapeDtypeStruct((TILE_DEV * SIDE, SIDE), f32),
            jax.ShapeDtypeStruct((DETECTORS_LOCAL, 1, BASELINE_COUNT), f32),
        ),
        in_specs=[hbm] * 7,
        out_specs=(vmem, vmem),
        scratch_shapes=[
            pltpu.SMEM((DETECTORS_LOCAL, 1, SEG_PER), i32),
            pltpu.SMEM((DETECTORS_LOCAL, 1, BASELINE_COUNT), i32),
            pltpu.VMEM((DETECTORS_LOCAL, SAMP_DEV), f32),
            pltpu.VMEM((DETECTORS_LOCAL, SAMP_DEV), i32),
            pltpu.VMEM((MODES, DETECTORS_LOCAL * groups), f32),
            pltpu.VMEM((MODES, MODES), f32),
            pltpu.VMEM((TILE_DEV * SIDE, SIDE), f32),
            pltpu.SMEM((groups,), i32),
            pltpu.VMEM((8 * groups, MODES), f32),
            pltpu.VMEM((8 * chunks, LANES), i32),
            pltpu.VMEM((8 * chunks, LANES), f32),
            pltpu.VMEM((8 * chunks, LANES), i32),
            pltpu.VMEM((ENTRIES, HALF, LANES), i32),
            pltpu.VMEM((ENTRIES, HALF, LANES), f32),
            pltpu.VMEM((8 * chunks, LANES), f32),
            pltpu.VMEM((8 * chunks, LANES), f32),
            pltpu.VMEM((8 * groups, LANES), f32),
            pltpu.VMEM((8 * groups, 8 * groups), f32),
            pltpu.VMEM((TILE_DEV * SIDE, SIDE), f32),
            pltpu.VMEM((TOGETHER, SIDE, SIDE), f32),
            pltpu.VMEM((TOGETHER, TERMS, HALF, LANES), f32),
            pltpu.VMEM((TILE_DEV, TERMS * ROWS, COLS), f32),
            pltpu.VMEM((groups * HALF // LANES, LANES, LANES), i32),
            pltpu.VMEM((groups, COLS // LANES, PART, LANES), bf16),
            pltpu.VMEM((groups, HALF, ROWS, LANES), bf16),
            pltpu.VMEM((groups, HALF, LANES), i32),
            pltpu.VMEM((groups, HALF, LANES), i32),
            pltpu.VMEM((ITERS, groups, HALF, LANES), bf16),
            pltpu.VMEM((ITERS, groups, HALF, LANES), bf16),
            pltpu.VMEM((ITERS, chunks, DETECTORS_LOCAL, LANES), f32),
            pltpu.VMEM((ITERS, groups, DETECTORS_LOCAL, LANES), f32),
            pltpu.VMEM((ITERS, groups, DETECTORS_LOCAL, LANES), f32),
            pltpu.VMEM((ITERS, chunks, DETECTORS_LOCAL, LANES), f32),
            pltpu.VMEM((ITERS, 8, LANES), f32),
            pltpu.VMEM((ITERS, blocks, 8, LANES), f32),
            pltpu.VMEM((ITERS, groups, HALF, LANES), f32),
            pltpu.VMEM((ITERS, groups, HALF, LANES), f32),
            pltpu.VMEM((DETECTORS_LOCAL, 1, LANES), f32),
            pltpu.VMEM((ITERS, groups, 1, LANES), f32),
            pltpu.VMEM((ITERS, groups, 1, LANES), f32),
            dma((7,)),
            dma((1 + 6 * ITERS,)),
            dma((groups,)),
            dma((ITERS,)),
            dma((ITERS,)),
            dma((ITERS,)),
            dma((ITERS,)),
            dma((ITERS, groups)),
            dma((ITERS, groups)),
        ],
        compiler_params=pltpu.CompilerParams(
            collective_id=0, has_side_effects=True, vmem_limit_bytes=VMEM_BYTES
        ),
    )(*(
        pltpu.with_memory_space_constraint(array, pltpu.HBM)
        for array in (
            crossings, lengths, detector_samples, pixels, mode_templates.T, mixing,
            sky_map.reshape(TILE_DEV * SIDE, SIDE),
        )
    ))
    return sky.reshape(TILE_DEV, SIDE, SIDE), fit


def solution(mesh):
    placed = (
        P("det", "tile"),
        P("det", "tile"),
        P("det", "tile", None),
        P("det", "tile", None),
        P(),
        P(),
        P(("det", "tile"), None, None),
    )
    return jax.shard_map(
        local,
        mesh=mesh,
        in_specs=placed,
        out_specs=(P(("det", "tile"), None, None), P("det", "tile", None)),
        check_vma=False,
    )
```

```python
import functools

import jax
import jax.numpy as jnp
from jax import lax
from jax.experimental import pallas as pl
from jax.experimental.pallas import tpu as pltpu
from jax.sharding import PartitionSpec as P

SIDE = 128
PIX = 16384
TILE_DEV = 2
MODES = 64
DETECTORS_LOCAL = 4
SAMP_DEV = 4096
SEG_PER = 4
BASELINE_COUNT = 16
ITERS = 2
PART = SAMP_DEV // SEG_PER
ENTRIES = DETECTORS_LOCAL * SEG_PER
LANES = 128
COLS = 256
ROWS = PIX // COLS
HALF = PART // LANES
TERMS = 3
SEG_BITS = 16
SEG_UNIT = 1 << SEG_BITS
TOGETHER = 4
VMEM_BYTES = 32 * 1024 * 1024

HUBER = 1.345
EPS = 1e-05
MESH = pl.DeviceIdType.MESH
ZRING = 8


def kernel(
    groups,
    blocks,
    cross_hbm,
    len_hbm,
    det_hbm,
    pix_hbm,
    templ_hbm,
    mixing_hbm,
    sky_hbm,
    sky_out,
    base_out,
    cross_ref,
    len_ref,
    det_ref,
    pix_ref,
    templ_ref,
    mixing_ref,
    current,
    ent_ref,
    code_h,
    det_h,
    seg_h,
    code_e,
    val_e,
    work,
    clean_h,
    stack,
    matrix,
    table,
    chosen,
    parts,
    acc,
    columns,
    coloh,
    rowoh,
    send_i,
    recv_i,
    send_a,
    recv_a,
    send_b,
    recv_b,
    send_c,
    recv_c,
    send_d,
    recv_d,
    send_e,
    recv_e,
    head,
    send_h,
    recv_h,
    load_sem,
    sent,
    sem_i,
    sem_a,
    sem_b,
    sem_c,
    sem_d,
    sem_e,
    sem_h,
):
    me = lax.axis_index("det")
    block = lax.axis_index("tile")
    chunks = SAMP_DEV // LANES
    detectors = groups * DETECTORS_LOCAL
    xring = groups // ZRING
    my_x, my_z = lax.div(me, ZRING), lax.rem(me, ZRING)

    loads = [
        pltpu.make_async_copy(src, dst, load_sem.at[i])
        for i, (src, dst) in enumerate(
            ((cross_hbm, cross_ref), (pix_hbm, pix_ref), (len_hbm, len_ref), (det_hbm, det_ref),
             (templ_hbm, templ_ref), (mixing_hbm, mixing_ref), (sky_hbm, current))
        )
    ]
    for load in loads:
        load.start()

    def hops(dx, dz):
        return min(dx, xring - dx) + min(dz, ZRING - dz)

    xs = [lax.rem(my_x + dx, xring) * ZRING for dx in range(xring)]
    zs = [lax.rem(my_z + dz, ZRING) for dz in range(ZRING)]
    offsets = sorted(
        ((dx, dz) for dx in range(xring) for dz in range(ZRING) if dx or dz), key=lambda o: hops(*o)
    )
    near = [xs[dx] + zs[dz] for dx, dz in offsets]
    far = near[::-1]

    def copy_to(src, dst, send_sem, recv_sem, **place):
        return pltpu.make_async_remote_copy(
            src_ref=src, dst_ref=dst, send_sem=send_sem, recv_sem=recv_sem,
            device_id=place, device_id_type=MESH,
        )

    def wait_bytes(ref, count, sem):
        view = ref.at[pl.ds(0, count)]
        pltpu.make_async_copy(view, view, sem).wait()

    barrier = pltpu.get_barrier_semaphore()
    for o in far:
        pl.semaphore_signal(barrier, inc=1, device_id={"det": o}, device_id_type=MESH)
    others = [lax.rem(block + step, blocks) for step in range(1, blocks)]
    for b in others:
        pl.semaphore_signal(barrier, inc=1, device_id={"tile": b}, device_id_type=MESH)

    loads[0].wait()
    def entry_place(e):
        return e // SEG_PER, e % SEG_PER

    tiles = [cross_ref[entry_place(e)[0], 0, entry_place(e)[1]] for e in range(ENTRIES)]
    owners = [lax.div(tile, TILE_DEV * blocks) for tile in tiles]

    def find_entry(o, carry):
        found = jnp.int32(-1)
        for e in range(ENTRIES):
            found = jnp.where(owners[e] == o, e, found)
        ent_ref[o] = found
        return carry

    lax.fori_loop(0, groups, find_entry, 0)

    def rows_of(j):
        return slice(DETECTORS_LOCAL * j, DETECTORS_LOCAL * (j + 1))

    loads[1].wait()
    for j in range(chunks):
        code_h[rows_of(j), :] = pix_ref[:, LANES * j : LANES * (j + 1)]

    loads[2].wait()
    home = (chunks * DETECTORS_LOCAL // 8, 8, LANES)
    flat = (chunks * DETECTORS_LOCAL, LANES)
    sublane = lax.broadcasted_iota(jnp.int32, (8, LANES), 0)
    position = (
        lax.broadcasted_iota(jnp.int32, home, 0) * (8 // DETECTORS_LOCAL)
        + lax.div(lax.broadcasted_iota(jnp.int32, home, 1), DETECTORS_LOCAL)
    ) * LANES + lax.broadcasted_iota(jnp.int32, home, 2)
    ends = [jnp.int32(0)] * DETECTORS_LOCAL
    seg = jnp.zeros(home, jnp.int32)
    for n in range(BASELINE_COUNT):
        end = jnp.zeros((8, LANES), jnp.int32)
        for l in range(DETECTORS_LOCAL):
            ends[l] = ends[l] + len_ref[l, 0, n]
            end = jnp.where(lax.rem(sublane, DETECTORS_LOCAL) == l, ends[l], end)
        seg += (position >= end[None]).astype(jnp.int32)
    seg_h[...] = seg.reshape(flat)

    def fold(tile):
        turned = jnp.concatenate([tile[DETECTORS_LOCAL:], tile[:DETECTORS_LOCAL]], axis=0)
        return tile + turned

    def entry_rows(e):
        l, k = entry_place(e)
        return pl.ds(DETECTORS_LOCAL * HALF * k + l, HALF, stride=DETECTORS_LOCAL)

    for e in range(ENTRIES):
        code_e[e] = (
            code_h[entry_rows(e), :]
            + lax.rem(tiles[e], TILE_DEV) * PIX
            + seg_h[entry_rows(e), :] * SEG_UNIT
        )

    def pack_codes(o, carry):
        e = ent_ref[o]
        rows = code_e[jnp.maximum(e, 0)]
        send_i[o] = jnp.where(jnp.full(rows.shape, e, jnp.int32) >= 0, rows, -1)
        return carry

    lax.fori_loop(0, groups, pack_codes, 0)
    recv_i[me] = send_i[me]
    for load in loads[3:]:
        load.wait()

    pl.semaphore_wait(barrier, groups - 1 + blocks - 1)
    for o in near:
        copy_to(send_i.at[o], recv_i.at[me], sent.at[0], sem_i.at[me], det=o).start()

    for j in range(chunks):
        det_h[rows_of(j), :] = det_ref[:, LANES * j : LANES * (j + 1)]
    table[...] = current[...].astype(jnp.bfloat16).astype(jnp.float32)
    templates = templ_ref[...].T
    mixed = jnp.dot(
        templates, mixing_ref[...],
        precision=lax.Precision.HIGHEST, preferred_element_type=jnp.float32,
    )
    whole = jnp.dot(
        mixed, templ_ref[...],
        precision=lax.Precision.HIGHEST, preferred_element_type=jnp.float32,
    )
    high = whole.astype(jnp.bfloat16)
    matrix[0:detectors, :] = high
    matrix[detectors:, :] = (whole - high.astype(jnp.float32)).astype(jnp.bfloat16)
    def turn_columns():
        column = jnp.bitwise_and(recv_i[...].reshape(groups * HALF, LANES), COLS - 1).T
        for part in range(groups * HALF // LANES):
            columns[part] = column[:, LANES * part : LANES * (part + 1)]

    def flags(part, first, last):
        def one(i, carry):
            d = LANES // HALF * part + i
            code = recv_i[d]
            row = jnp.where(
                code < 0, -1, jnp.bitwise_and(lax.shift_right_arithmetic(code, 8), ROWS - 1)
            )
            square = (LANES, LANES)
            lane = lax.broadcasted_iota(jnp.int32, square, 1)
            for q in range(HALF):
                rowoh[d, q] = (
                    jnp.broadcast_to(row[q : q + 1, :], (ROWS, LANES))
                    == lax.broadcasted_iota(jnp.int32, (ROWS, LANES), 0)
                ).astype(jnp.float32).astype(jnp.bfloat16)
                col = jnp.take_along_axis(
                    columns[part], jnp.full(square, HALF * i + q, jnp.int32), axis=1
                )
                for h in range(COLS // LANES):
                    coloh[d, h, LANES * q : LANES * (q + 1), :] = (
                        col == lane + LANES * h
                    ).astype(jnp.float32).astype(jnp.bfloat16)
            return carry

        lax.fori_loop(first, last, one, 0)

    def zigzag(i, size):
        return size // 2 + lax.div(i + 1, 2) * (1 - 2 * lax.rem(i, 2))

    def far_peer(step):
        x = lax.rem(my_x + zigzag(lax.rem(step, xring), xring), xring)
        z = lax.rem(my_z + zigzag(lax.div(step, xring), ZRING), ZRING)
        return x * ZRING + z

    def near_peer(step):
        return far_peer(groups - 1 - step)

    baseline = jnp.zeros((8, LANES), jnp.float32)

    for it in range(ITERS):
        base_sem = 1 + 6 * it

        def answer(batch, carry):
            slots = [
                near_peer(step) if it == 0 else far_peer(step)
                for step in (TOGETHER * batch + i for i in range(TOGETHER))
            ]
            if it == 0:
                for i, d in enumerate(slots):
                    @pl.when(TOGETHER * batch + i > 0)
                    def _():
                        copy_to(
                            send_i.at[d], recv_i.at[d], sent.at[0], sem_i.at[d], det=d
                        ).wait_recv()
            values = []
            for i, d in enumerate(slots):
                code = recv_i[d]
                row = jnp.bitwise_and(lax.shift_right_arithmetic(code, 7), SIDE - 1)
                col = jnp.bitwise_and(code, LANES - 1)
                second = jnp.bitwise_and(code, PIX) > 0
                for g in range(SIDE // 8):
                    chosen[i, 8 * g : 8 * g + 8, :] = jnp.where(
                        second,
                        table[SIDE + 8 * g : SIDE + 8 * g + 8, :],
                        table[8 * g : 8 * g + 8, :],
                    )
                value = jnp.zeros((HALF, LANES), jnp.float32)
                for r in range(SIDE):
                    line = jnp.broadcast_to(chosen[i, r : r + 1, :], (HALF, LANES))
                    value = jnp.where(row == r, jnp.take_along_axis(line, col, axis=1), value)
                values.append(value)
            for d, value in zip(slots, values):
                send_a[it, d] = value.astype(jnp.bfloat16)
            for d in slots:
                @pl.when(d != me)
                def _():
                    copy_to(
                        send_a.at[it, d], recv_a.at[it, me], sent.at[base_sem], sem_a.at[it], det=d
                    ).start()

            return carry

        lax.fori_loop(0, groups // TOGETHER, answer, 0)
        recv_a[it, me] = send_a[it, me]
        if it == 0:
            turn_columns()
            flags(0, 0, 8)
        wait_bytes(recv_a.at[it], groups - 1, sem_a.at[it])

        for e in range(ENTRIES):
            work[entry_rows(e), :] = recv_a[it, owners[e]].astype(jnp.float32)
        residual = det_h[...] - work[...]
        for j in range(chunks):
            send_b[it, j] = residual[rows_of(j), :]
        recv_b[it, me] = send_b[it, me]
        for j in far:
            copy_to(
                send_b.at[it, j], recv_b.at[it, me], sent.at[base_sem + 1], sem_b.at[it], det=j
            ).start()
        if it == 0:
            flags(0, 8, 16)
            flags(1, 0, 4)
        wait_bytes(recv_b.at[it], groups - 1, sem_b.at[it])

        for d in range(groups):
            stack[rows_of(d), :] = recv_b[it, d]
        every = stack[...]
        high = every.astype(jnp.bfloat16)
        low = (every - high.astype(jnp.float32)).astype(jnp.bfloat16)
        both = jnp.dot(matrix[...], high, preferred_element_type=jnp.float32)
        every = every - (
            both[0:detectors, :]
            + both[detectors:, :]
            + jnp.dot(matrix[0:detectors, :], low, preferred_element_type=jnp.float32)
        )
        for d in range(groups):
            send_c[it, d] = every[rows_of(d), :]
        recv_c[it, me] = send_c[it, me]
        for d in far:
            copy_to(
                send_c.at[it, d], recv_c.at[it, me], sent.at[base_sem + 2], sem_c.at[it], det=d
            ).start()
        acc[...] = jnp.zeros_like(acc)
        if it == 0:
            flags(1, 4, 16)
        wait_bytes(recv_c.at[it], groups - 1, sem_c.at[it])

        for j in range(chunks):
            clean_h[rows_of(j), :] = recv_c[it, j]
        cleaned = clean_h[...].reshape(home)
        send_d[it] = jnp.sum(cleaned * cleaned, axis=0)
        recv_d[it, block] = send_d[it]
        for b in others:
            copy_to(
                send_d.at[it], recv_d.at[it, block], sent.at[base_sem + 3], sem_d.at[it], tile=b
            ).start()
        for e in range(ENTRIES):
            val_e[e] = clean_h[entry_rows(e), :]
        for o in near:
            send_e[it, o] = val_e[jnp.maximum(ent_ref[o], 0)]
            copy_to(
                send_e.at[it, o], recv_e.at[it, me], sent.at[base_sem + 4], sem_e.at[it, me], det=o
            ).start()
        recv_e[it, me] = val_e[jnp.maximum(ent_ref[me], 0)]
        wait_bytes(recv_d.at[it], blocks - 1, sem_d.at[it])
        squares = fold(jnp.sum(recv_d[it], axis=0))
        squares = jnp.sum(squares, axis=1, keepdims=True)
        level = HUBER * jnp.sqrt(squares / (SAMP_DEV * blocks) + EPS)
        weight = level[None] / jnp.maximum(jnp.abs(cleaned), level[None])
        weighted = weight * cleaned
        seg = seg_h[...].reshape(home)
        lane = lax.broadcasted_iota(jnp.int32, (8, LANES), 1)
        numerator = jnp.zeros((8, LANES), jnp.float32)
        denominator = jnp.zeros((8, LANES), jnp.float32)
        for n in range(BASELINE_COUNT):
            inside = seg == n
            numerator = jnp.where(
                lane == n,
                jnp.sum(jnp.sum(jnp.where(inside, weighted, 0.0), axis=0), axis=1, keepdims=True),
                numerator,
            )
            denominator = jnp.where(
                lane == n,
                jnp.sum(jnp.sum(jnp.where(inside, weight, 0.0), axis=0), axis=1, keepdims=True),
                denominator,
            )
        denominator = fold(denominator)
        increment = fold(numerator) / jnp.where(denominator > 0.0, denominator, 1.0)
        line = jnp.where(lane == BASELINE_COUNT, level, increment)
        for l in range(DETECTORS_LOCAL):
            head[l] = line[l : l + 1, :]
        for o in near:
            send_h[it, o] = head[lax.div(jnp.maximum(ent_ref[o], 0), SEG_PER)]
            copy_to(
                send_h.at[it, o], recv_h.at[it, me], sent.at[base_sem + 5], sem_h.at[it, me], det=o
            ).start()
        recv_h[it, me] = head[lax.div(jnp.maximum(ent_ref[me], 0), SEG_PER)]
        baseline = baseline + increment
        if it + 1 < ITERS:
            stepped = jnp.zeros(home, jnp.float32)
            for n in range(BASELINE_COUNT):
                stepped = jnp.where(seg == n, increment[:, n : n + 1][None], stepped)
            det_h[...] = det_h[...] - stepped.reshape(flat)

        def collect(batch, carry):
            slots = [near_peer(TOGETHER * batch + i) for i in range(TOGETHER)]
            for i, d in enumerate(slots):
                @pl.when(TOGETHER * batch + i > 0)
                def _():
                    copy_to(
                        send_e.at[it, d], recv_e.at[it, d], sent.at[base_sem + 4], sem_e.at[it, d],
                        det=d,
                    ).wait_recv()
                    copy_to(
                        send_h.at[it, d], recv_h.at[it, d], sent.at[base_sem + 5], sem_h.at[it, d],
                        det=d,
                    ).wait_recv()
            for i, d in enumerate(slots):
                cleaned_d = recv_e[it, d]
                line = jnp.broadcast_to(recv_h[it, d], (HALF, LANES))
                seg_d = jnp.bitwise_and(
                    lax.shift_right_arithmetic(recv_i[d], SEG_BITS), BASELINE_COUNT - 1
                )
                step_d = jnp.take_along_axis(line, seg_d, axis=1)
                level_d = jnp.take_along_axis(
                    line, jnp.full((HALF, LANES), BASELINE_COUNT, jnp.int32), axis=1
                )
                weight_d = level_d / jnp.maximum(jnp.abs(cleaned_d), level_d)
                value_d = weight_d * (cleaned_d - step_d)
                high = value_d.astype(jnp.bfloat16).astype(jnp.float32)
                parts[i, 0] = high
                parts[i, 1] = value_d - high
                parts[i, 2] = weight_d
            sums = []
            for i, d in enumerate(slots):
                weighed = jnp.concatenate(
                    [
                        jnp.concatenate(
                            [
                                rowoh[d, q]
                                * jnp.broadcast_to(
                                    parts[i, t, q : q + 1, :], (ROWS, LANES)
                                ).astype(jnp.bfloat16)
                                for t in range(TERMS)
                            ],
                            axis=0,
                        )
                        for q in range(HALF)
                    ],
                    axis=1,
                )
                spread = jnp.concatenate([coloh[d, h] for h in range(COLS // LANES)], axis=1)
                product = jnp.dot(weighed, spread, preferred_element_type=jnp.float32)
                second = (
                    jnp.broadcast_to(jnp.bitwise_and(recv_i[d], PIX)[0:1, 0:1], product.shape) > 0
                )
                sums.append((jnp.where(second, 0.0, product), jnp.where(second, product, 0.0)))
            for t in range(TILE_DEV):
                total = sums[0][t]
                for part in sums[1:]:
                    total = total + part[t]
                acc[t] += total
            return carry

        lax.fori_loop(0, groups // TOGETHER, collect, 0)
        for t in range(TILE_DEV):
            change = (acc[t, 0:ROWS, :] + acc[t, ROWS : 2 * ROWS, :]) / jnp.maximum(
                acc[t, 2 * ROWS : 3 * ROWS, :], 1.0
            )
            for half in range(2):
                rows = pl.ds(SIDE * t + half, ROWS, stride=2)
                current[rows, :] = current[rows, :] + change[:, LANES * half : LANES * (half + 1)]
        if it + 1 < ITERS:
            table[...] = current[...].astype(jnp.bfloat16).astype(jnp.float32)

    sky_out[...] = current[...]
    for l in range(DETECTORS_LOCAL):
        base_out[l] = baseline[l : l + 1, 0:BASELINE_COUNT]

    wait_bytes(send_i, groups - 1, sent.at[0])
    for it in range(ITERS):
        base_sem = 1 + 6 * it
        wait_bytes(send_a.at[it], groups - 1, sent.at[base_sem])
        wait_bytes(send_b.at[it], groups - 1, sent.at[base_sem + 1])
        wait_bytes(send_c.at[it], groups - 1, sent.at[base_sem + 2])
        wait_bytes(recv_d.at[it], blocks - 1, sent.at[base_sem + 3])
        wait_bytes(send_e.at[it], groups - 1, sent.at[base_sem + 4])
        wait_bytes(send_h.at[it], groups - 1, sent.at[base_sem + 5])


def local(detector_samples, pixels, crossings, lengths, mode_templates, mixing, sky_map):
    groups = lax.axis_size("det")
    blocks = lax.axis_size("tile")
    chunks = SAMP_DEV // LANES
    vmem = pl.BlockSpec(memory_space=pltpu.VMEM)
    hbm = pl.BlockSpec(memory_space=pltpu.HBM)
    f32, bf16, i32 = jnp.float32, jnp.bfloat16, jnp.int32
    dma = pltpu.SemaphoreType.DMA
    sky, fit = pl.pallas_call(
        functools.partial(kernel, groups, blocks),
        out_shape=(
            jax.ShapeDtypeStruct((TILE_DEV * SIDE, SIDE), f32),
            jax.ShapeDtypeStruct((DETECTORS_LOCAL, 1, BASELINE_COUNT), f32),
        ),
        in_specs=[hbm] * 7,
        out_specs=(vmem, vmem),
        scratch_shapes=[
            pltpu.SMEM((DETECTORS_LOCAL, 1, SEG_PER), i32),
            pltpu.SMEM((DETECTORS_LOCAL, 1, BASELINE_COUNT), i32),
            pltpu.VMEM((DETECTORS_LOCAL, SAMP_DEV), f32),
            pltpu.VMEM((DETECTORS_LOCAL, SAMP_DEV), i32),
            pltpu.VMEM((MODES, DETECTORS_LOCAL * groups), f32),
            pltpu.VMEM((MODES, MODES), f32),
            pltpu.VMEM((TILE_DEV * SIDE, SIDE), f32),
            pltpu.SMEM((groups,), i32),
            pltpu.VMEM((DETECTORS_LOCAL * chunks, LANES), i32),
            pltpu.VMEM((DETECTORS_LOCAL * chunks, LANES), f32),
            pltpu.VMEM((DETECTORS_LOCAL * chunks, LANES), i32),
            pltpu.VMEM((ENTRIES, HALF, LANES), i32),
            pltpu.VMEM((ENTRIES, HALF, LANES), f32),
            pltpu.VMEM((DETECTORS_LOCAL * chunks, LANES), f32),
            pltpu.VMEM((DETECTORS_LOCAL * chunks, LANES), f32),
            pltpu.VMEM((DETECTORS_LOCAL * groups, LANES), f32),
            pltpu.VMEM((2 * DETECTORS_LOCAL * groups, DETECTORS_LOCAL * groups), bf16),
            pltpu.VMEM((TILE_DEV * SIDE, SIDE), f32),
            pltpu.VMEM((TOGETHER, SIDE, SIDE), f32),
            pltpu.VMEM((TOGETHER, TERMS, HALF, LANES), f32),
            pltpu.VMEM((TILE_DEV, TERMS * ROWS, COLS), f32),
            pltpu.VMEM((groups * HALF // LANES, LANES, LANES), i32),
            pltpu.VMEM((groups, COLS // LANES, PART, LANES), bf16),
            pltpu.VMEM((groups, HALF, ROWS, LANES), bf16),
            pltpu.VMEM((groups, HALF, LANES), i32),
            pltpu.VMEM((groups, HALF, LANES), i32),
            pltpu.VMEM((ITERS, groups, HALF, LANES), bf16),
            pltpu.VMEM((ITERS, groups, HALF, LANES), bf16),
            pltpu.VMEM((ITERS, chunks, DETECTORS_LOCAL, LANES), f32),
            pltpu.VMEM((ITERS, groups, DETECTORS_LOCAL, LANES), f32),
            pltpu.VMEM((ITERS, groups, DETECTORS_LOCAL, LANES), f32),
            pltpu.VMEM((ITERS, chunks, DETECTORS_LOCAL, LANES), f32),
            pltpu.VMEM((ITERS, 8, LANES), f32),
            pltpu.VMEM((ITERS, blocks, 8, LANES), f32),
            pltpu.VMEM((ITERS, groups, HALF, LANES), f32),
            pltpu.VMEM((ITERS, groups, HALF, LANES), f32),
            pltpu.VMEM((DETECTORS_LOCAL, 1, LANES), f32),
            pltpu.VMEM((ITERS, groups, 1, LANES), f32),
            pltpu.VMEM((ITERS, groups, 1, LANES), f32),
            dma((7,)),
            dma((1 + 6 * ITERS,)),
            dma((groups,)),
            dma((ITERS,)),
            dma((ITERS,)),
            dma((ITERS,)),
            dma((ITERS,)),
            dma((ITERS, groups)),
            dma((ITERS, groups)),
        ],
        compiler_params=pltpu.CompilerParams(
            collective_id=0, has_side_effects=True, vmem_limit_bytes=VMEM_BYTES
        ),
    )(*(
        pltpu.with_memory_space_constraint(array, pltpu.HBM)
        for array in (
            crossings, lengths, detector_samples, pixels, mode_templates.T, mixing,
            sky_map.reshape(TILE_DEV * SIDE, SIDE),
        )
    ))
    return sky.reshape(TILE_DEV, SIDE, SIDE), fit


def solution(mesh):
    placed = (
        P("det", "tile"),
        P("det", "tile"),
        P("det", "tile", None),
        P("det", "tile", None),
        P(),
        P(),
        P(("det", "tile"), None, None),
    )
    return jax.shard_map(
        local,
        mesh=mesh,
        in_specs=placed,
        out_specs=(P(("det", "tile"), None, None), P("det", "tile", None)),
        check_vma=False,
    )
```

```python
import functools

import jax
import jax.numpy as jnp
from jax import lax
from jax.experimental import pallas as pl
from jax.experimental.pallas import tpu as pltpu
from jax.sharding import PartitionSpec as P

SIDE = 128
PIX = 16384
TILE_DEV = 2
MODES = 64
DETECTORS_LOCAL = 4
SAMP_DEV = 4096
SEG_PER = 4
BASELINE_COUNT = 16
ITERS = 2
PART = SAMP_DEV // SEG_PER
ENTRIES = DETECTORS_LOCAL * SEG_PER
LANES = 128
COLS = 256
ROWS = PIX // COLS
HALF = PART // LANES
TERMS = 4
TOGETHER = 4
MANY = 8
VMEM_BYTES = 32 * 1024 * 1024

HUBER = 1.345
EPS = 1e-05
MESH = pl.DeviceIdType.MESH
ZRING = 8


def kernel(
    groups,
    blocks,
    cross_hbm,
    len_hbm,
    det_hbm,
    pix_hbm,
    templ_hbm,
    mixing_hbm,
    sky_hbm,
    sky_out,
    base_out,
    cross_ref,
    len_ref,
    det_ref,
    pix_ref,
    templ_ref,
    mixing_ref,
    current,
    ent_ref,
    code_h,
    det_h,
    seg_h,
    code_e,
    val_e,
    work,
    clean_h,
    stack,
    matrix,
    table,
    chosen,
    parts,
    acc,
    columns,
    coloh,
    rowoh,
    send_i,
    recv_i,
    seg_e,
    send_s,
    recv_s,
    code_g,
    send_a,
    recv_a,
    send_b,
    recv_b,
    send_c,
    recv_c,
    send_d,
    recv_d,
    send_e,
    recv_e,
    head,
    send_h,
    recv_h,
    load_sem,
    sent,
    sem_i,
    sem_s,
    sem_a,
    sem_b,
    sem_c,
    sem_d,
    sem_e,
    sem_h,
):
    me = lax.axis_index("det")
    block = lax.axis_index("tile")
    chunks = SAMP_DEV // LANES
    detectors = groups * DETECTORS_LOCAL
    xring = groups // ZRING
    my_x, my_z = lax.div(me, ZRING), lax.rem(me, ZRING)

    loads = [
        pltpu.make_async_copy(src, dst, load_sem.at[i])
        for i, (src, dst) in enumerate(
            ((cross_hbm, cross_ref), (pix_hbm, pix_ref), (len_hbm, len_ref), (det_hbm, det_ref),
             (templ_hbm, templ_ref), (mixing_hbm, mixing_ref), (sky_hbm, current))
        )
    ]
    for load in loads:
        load.start()

    def hops(dx, dz):
        return min(dx, xring - dx) + min(dz, ZRING - dz)

    xs = [lax.rem(my_x + dx, xring) * ZRING for dx in range(xring)]
    zs = [lax.rem(my_z + dz, ZRING) for dz in range(ZRING)]
    offsets = sorted(
        ((dx, dz) for dx in range(xring) for dz in range(ZRING) if dx or dz), key=lambda o: hops(*o)
    )
    near = [xs[dx] + zs[dz] for dx, dz in offsets]
    far = near[::-1]

    def copy_to(src, dst, send_sem, recv_sem, **place):
        return pltpu.make_async_remote_copy(
            src_ref=src, dst_ref=dst, send_sem=send_sem, recv_sem=recv_sem,
            device_id=place, device_id_type=MESH,
        )

    def wait_bytes(ref, count, sem):
        view = ref.at[pl.ds(0, count)]
        pltpu.make_async_copy(view, view, sem).wait()

    barrier = pltpu.get_barrier_semaphore()
    for o in far:
        pl.semaphore_signal(barrier, inc=1, device_id={"det": o}, device_id_type=MESH)
    others = [lax.rem(block + step, blocks) for step in range(1, blocks)]
    for b in others:
        pl.semaphore_signal(barrier, inc=1, device_id={"tile": b}, device_id_type=MESH)

    loads[0].wait()
    def entry_place(e):
        return e // SEG_PER, e % SEG_PER

    tiles = [cross_ref[entry_place(e)[0], 0, entry_place(e)[1]] for e in range(ENTRIES)]
    owners = [lax.div(tile, TILE_DEV * blocks) for tile in tiles]

    def find_entry(o, carry):
        found = jnp.int32(-1)
        for e in range(ENTRIES):
            found = jnp.where(owners[e] == o, e, found)
        ent_ref[o] = found
        return carry

    lax.fori_loop(0, groups, find_entry, 0)

    def rows_of(j):
        return slice(DETECTORS_LOCAL * j, DETECTORS_LOCAL * (j + 1))

    loads[1].wait()
    for j in range(chunks):
        code_h[rows_of(j), :] = pix_ref[:, LANES * j : LANES * (j + 1)]

    loads[2].wait()
    home = (chunks * DETECTORS_LOCAL // 8, 8, LANES)
    flat = (chunks * DETECTORS_LOCAL, LANES)
    sublane = lax.broadcasted_iota(jnp.int32, (8, LANES), 0)
    position = (
        lax.broadcasted_iota(jnp.int32, home, 0) * (8 // DETECTORS_LOCAL)
        + lax.div(lax.broadcasted_iota(jnp.int32, home, 1), DETECTORS_LOCAL)
    ) * LANES + lax.broadcasted_iota(jnp.int32, home, 2)
    ends = [jnp.int32(0)] * DETECTORS_LOCAL
    seg = jnp.zeros(home, jnp.int32)
    for n in range(BASELINE_COUNT):
        end = jnp.zeros((8, LANES), jnp.int32)
        for l in range(DETECTORS_LOCAL):
            ends[l] = ends[l] + len_ref[l, 0, n]
            end = jnp.where(lax.rem(sublane, DETECTORS_LOCAL) == l, ends[l], end)
        seg += (position >= end[None]).astype(jnp.int32)
    seg_h[...] = seg.reshape(flat)

    def fold(tile):
        turned = jnp.concatenate([tile[DETECTORS_LOCAL:], tile[:DETECTORS_LOCAL]], axis=0)
        return tile + turned

    def entry_rows(e):
        l, k = entry_place(e)
        return pl.ds(DETECTORS_LOCAL * HALF * k + l, HALF, stride=DETECTORS_LOCAL)

    for e in range(ENTRIES):
        code_e[e] = (
            code_h[entry_rows(e), :]
            + lax.rem(tiles[e], TILE_DEV) * PIX
        )
        seg_e[e] = seg_h[entry_rows(e), :].astype(jnp.int16)

    def pack_codes(o, carry):
        e = ent_ref[o]
        rows = code_e[jnp.maximum(e, 0)]
        send_i[o] = jnp.where(jnp.full(rows.shape, e, jnp.int32) >= 0, rows, -1).astype(jnp.int16)
        return carry

    lax.fori_loop(0, groups, pack_codes, 0)
    recv_i[me] = send_i[me]
    for load in loads[3:]:
        load.wait()

    pl.semaphore_wait(barrier, groups - 1 + blocks - 1)
    for o in near:
        copy_to(send_i.at[o], recv_i.at[me], sent.at[0], sem_i.at[me], det=o).start()

    for o in near:
        send_s[o] = seg_e[jnp.maximum(ent_ref[o], 0)]
        copy_to(send_s.at[o], recv_s.at[me], sent.at[1], sem_s, det=o).start()
    recv_s[me] = seg_e[jnp.maximum(ent_ref[me], 0)]

    for j in range(chunks):
        det_h[rows_of(j), :] = det_ref[:, LANES * j : LANES * (j + 1)]
    table[...] = current[...].astype(jnp.bfloat16).astype(jnp.float32)
    templates = templ_ref[...].T
    mixed = jnp.dot(
        templates, mixing_ref[...],
        precision=lax.Precision.HIGHEST, preferred_element_type=jnp.float32,
    )
    whole = jnp.dot(
        mixed, templ_ref[...],
        precision=lax.Precision.HIGHEST, preferred_element_type=jnp.float32,
    )
    high = whole.astype(jnp.bfloat16)
    matrix[0:detectors, :] = high
    matrix[detectors:, :] = (whole - high.astype(jnp.float32)).astype(jnp.bfloat16)
    def turn_columns():
        column = jnp.bitwise_and(code_g[...].reshape(groups * HALF, LANES), COLS - 1).T
        for part in range(groups * HALF // LANES):
            columns[part] = column[:, LANES * part : LANES * (part + 1)]

    def flags(part, first, last):
        def one(i, carry):
            d = LANES // HALF * part + i
            code = code_g[d]
            row = jnp.where(
                code < 0, -1, jnp.bitwise_and(lax.shift_right_arithmetic(code, 8), ROWS - 1)
            )
            square = (LANES, LANES)
            lane = lax.broadcasted_iota(jnp.int32, square, 1)
            for q in range(HALF):
                rowoh[d, q] = (
                    jnp.broadcast_to(row[q : q + 1, :], (ROWS, LANES))
                    == lax.broadcasted_iota(jnp.int32, (ROWS, LANES), 0)
                ).astype(jnp.float32).astype(jnp.bfloat16)
                col = jnp.take_along_axis(
                    columns[part], jnp.full(square, HALF * i + q, jnp.int32), axis=1
                )
                for h in range(COLS // LANES):
                    coloh[d, h, LANES * q : LANES * (q + 1), :] = (
                        col == lane + LANES * h
                    ).astype(jnp.float32).astype(jnp.bfloat16)
            return carry

        lax.fori_loop(first, last, one, 0)

    def zigzag(i, size):
        return size // 2 + lax.div(i + 1, 2) * (1 - 2 * lax.rem(i, 2))

    def far_peer(step):
        x = lax.rem(my_x + zigzag(lax.rem(step, xring), xring), xring)
        z = lax.rem(my_z + zigzag(lax.div(step, xring), ZRING), ZRING)
        return x * ZRING + z

    def near_peer(step):
        return far_peer(groups - 1 - step)

    baseline = jnp.zeros((8, LANES), jnp.float32)

    for it in range(ITERS):
        base_sem = 2 + 6 * it

        def answer(batch, carry):
            slots = [
                near_peer(step) if it == 0 else far_peer(step)
                for step in (TOGETHER * batch + i for i in range(TOGETHER))
            ]
            if it == 0:
                for i, d in enumerate(slots):
                    @pl.when(TOGETHER * batch + i > 0)
                    def _():
                        copy_to(
                            send_i.at[d], recv_i.at[d], sent.at[0], sem_i.at[d], det=d
                        ).wait_recv()
            values = []
            for i, d in enumerate(slots):
                if it == 0:
                    code_g[d] = recv_i[d].astype(jnp.int32)
                code = code_g[d]
                row = jnp.bitwise_and(lax.shift_right_arithmetic(code, 7), SIDE - 1)
                col = jnp.bitwise_and(code, LANES - 1)
                second = jnp.bitwise_and(code, PIX) > 0
                for g in range(SIDE // 8):
                    chosen[i, 8 * g : 8 * g + 8, :] = jnp.where(
                        second,
                        table[SIDE + 8 * g : SIDE + 8 * g + 8, :],
                        table[8 * g : 8 * g + 8, :],
                    )
                value = jnp.zeros((HALF, LANES), jnp.float32)
                for r in range(SIDE):
                    line = jnp.broadcast_to(chosen[i, r : r + 1, :], (HALF, LANES))
                    value = jnp.where(row == r, jnp.take_along_axis(line, col, axis=1), value)
                values.append(value)
            for d, value in zip(slots, values):
                send_a[it, d] = value.astype(jnp.bfloat16)
            for d in slots:
                @pl.when(d != me)
                def _():
                    copy_to(
                        send_a.at[it, d], recv_a.at[it, me], sent.at[base_sem], sem_a.at[it], det=d
                    ).start()

            return carry

        lax.fori_loop(0, groups // TOGETHER, answer, 0)
        recv_a[it, me] = send_a[it, me]
        if it == 0:
            turn_columns()
            flags(0, 0, 8)
        wait_bytes(recv_a.at[it], groups - 1, sem_a.at[it])

        for e in range(ENTRIES):
            work[entry_rows(e), :] = recv_a[it, owners[e]].astype(jnp.float32)
        residual = det_h[...] - work[...]
        for j in range(chunks):
            send_b[it, j] = residual[rows_of(j), :]
        recv_b[it, me] = send_b[it, me]
        for j in far:
            copy_to(
                send_b.at[it, j], recv_b.at[it, me], sent.at[base_sem + 1], sem_b.at[it], det=j
            ).start()
        if it == 0:
            flags(0, 8, 16)
            flags(1, 0, 4)
        wait_bytes(recv_b.at[it], groups - 1, sem_b.at[it])

        for d in range(groups):
            stack[rows_of(d), :] = recv_b[it, d]
        every = stack[...]
        high = every.astype(jnp.bfloat16)
        low = (every - high.astype(jnp.float32)).astype(jnp.bfloat16)
        both = jnp.dot(matrix[...], high, preferred_element_type=jnp.float32)
        every = every - (
            both[0:detectors, :]
            + both[detectors:, :]
            + jnp.dot(matrix[0:detectors, :], low, preferred_element_type=jnp.float32)
        )
        for d in range(groups):
            send_c[it, d] = every[rows_of(d), :]
        recv_c[it, me] = send_c[it, me]
        for d in far:
            copy_to(
                send_c.at[it, d], recv_c.at[it, me], sent.at[base_sem + 2], sem_c.at[it], det=d
            ).start()
        acc[...] = jnp.zeros_like(acc)
        if it == 0:
            flags(1, 4, 16)
        wait_bytes(recv_c.at[it], groups - 1, sem_c.at[it])

        for j in range(chunks):
            clean_h[rows_of(j), :] = recv_c[it, j]
        cleaned = clean_h[...].reshape(home)
        send_d[it] = jnp.sum(cleaned * cleaned, axis=0)
        recv_d[it, block] = send_d[it]
        for b in others:
            copy_to(
                send_d.at[it], recv_d.at[it, block], sent.at[base_sem + 3], sem_d.at[it], tile=b
            ).start()
        for e in range(ENTRIES):
            val_e[e] = clean_h[entry_rows(e), :]
        for o in near:
            send_e[it, o] = val_e[jnp.maximum(ent_ref[o], 0)]
            copy_to(
                send_e.at[it, o], recv_e.at[it, me], sent.at[base_sem + 4], sem_e.at[it, me], det=o
            ).start()
        recv_e[it, me] = val_e[jnp.maximum(ent_ref[me], 0)]
        wait_bytes(recv_d.at[it], blocks - 1, sem_d.at[it])
        squares = fold(jnp.sum(recv_d[it], axis=0))
        squares = jnp.sum(squares, axis=1, keepdims=True)
        level = HUBER * jnp.sqrt(squares / (SAMP_DEV * blocks) + EPS)
        weight = level[None] / jnp.maximum(jnp.abs(cleaned), level[None])
        weighted = weight * cleaned
        seg = seg_h[...].reshape(home)
        lane = lax.broadcasted_iota(jnp.int32, (8, LANES), 1)
        numerator = jnp.zeros((8, LANES), jnp.float32)
        denominator = jnp.zeros((8, LANES), jnp.float32)
        for n in range(BASELINE_COUNT):
            inside = seg == n
            numerator = jnp.where(
                lane == n,
                jnp.sum(jnp.sum(jnp.where(inside, weighted, 0.0), axis=0), axis=1, keepdims=True),
                numerator,
            )
            denominator = jnp.where(
                lane == n,
                jnp.sum(jnp.sum(jnp.where(inside, weight, 0.0), axis=0), axis=1, keepdims=True),
                denominator,
            )
        denominator = fold(denominator)
        increment = fold(numerator) / jnp.where(denominator > 0.0, denominator, 1.0)
        line = jnp.where(lane == BASELINE_COUNT, level, increment)
        for l in range(DETECTORS_LOCAL):
            head[l] = line[l : l + 1, :]
        for o in near:
            send_h[it, o] = head[lax.div(jnp.maximum(ent_ref[o], 0), SEG_PER)]
            copy_to(
                send_h.at[it, o], recv_h.at[it, me], sent.at[base_sem + 5], sem_h.at[it, me], det=o
            ).start()
        recv_h[it, me] = head[lax.div(jnp.maximum(ent_ref[me], 0), SEG_PER)]
        baseline = baseline + increment
        if it + 1 < ITERS:
            stepped = jnp.zeros(home, jnp.float32)
            for n in range(BASELINE_COUNT):
                stepped = jnp.where(seg == n, increment[:, n : n + 1][None], stepped)
            det_h[...] = det_h[...] - stepped.reshape(flat)

        if it == 0:
            wait_bytes(recv_s, groups - 1, sem_s)

        def collect(first, count):
            slots = [near_peer(first + i) for i in range(count)]
            for i, d in enumerate(slots):
                @pl.when(d != me)
                def _():
                    copy_to(
                        send_e.at[it, d], recv_e.at[it, d], sent.at[base_sem + 4], sem_e.at[it, d],
                        det=d,
                    ).wait_recv()
                    copy_to(
                        send_h.at[it, d], recv_h.at[it, d], sent.at[base_sem + 5], sem_h.at[it, d],
                        det=d,
                    ).wait_recv()
            for i, d in enumerate(slots):
                cleaned_d = recv_e[it, d]
                line = jnp.broadcast_to(recv_h[it, d], (HALF, LANES))
                seg_d = recv_s[d].astype(jnp.int32)
                step_d = jnp.take_along_axis(line, seg_d, axis=1)
                level_d = jnp.take_along_axis(
                    line, jnp.full((HALF, LANES), BASELINE_COUNT, jnp.int32), axis=1
                )
                weight_d = level_d / jnp.maximum(jnp.abs(cleaned_d), level_d)
                value_d = weight_d * (cleaned_d - step_d)
                high = value_d.astype(jnp.bfloat16).astype(jnp.float32)
                parts[i, 0] = high
                parts[i, 1] = value_d - high
                high = weight_d.astype(jnp.bfloat16).astype(jnp.float32)
                parts[i, 2] = high
                parts[i, 3] = weight_d - high
            sums = []
            for i, d in enumerate(slots):
                weighed = jnp.concatenate(
                    [
                        jnp.concatenate(
                            [
                                rowoh[d, q]
                                * jnp.broadcast_to(
                                    parts[i, t, q : q + 1, :], (ROWS, LANES)
                                ).astype(jnp.bfloat16)
                                for t in range(TERMS)
                            ],
                            axis=0,
                        )
                        for q in range(HALF)
                    ],
                    axis=1,
                )
                spread = jnp.concatenate([coloh[d, h] for h in range(COLS // LANES)], axis=1)
                product = jnp.dot(weighed, spread, preferred_element_type=jnp.float32)
                second = (
                    jnp.broadcast_to(jnp.bitwise_and(code_g[d], PIX)[0:1, 0:1], product.shape) > 0
                )
                sums.append((jnp.where(second, 0.0, product), jnp.where(second, product, 0.0)))
            for t in range(TILE_DEV):
                total = sums[0][t]
                for part in sums[1:]:
                    total = total + part[t]
                acc[t] += total

        def collect_many(batch, carry):
            collect(TOGETHER + MANY * batch, MANY)
            return carry

        collect(0, TOGETHER)
        many = (groups - TOGETHER) // MANY
        lax.fori_loop(0, many, collect_many, 0)
        rest = TOGETHER + MANY * many
        if rest < groups:
            collect(rest, groups - rest)
        for t in range(TILE_DEV):
            change = (acc[t, 0:ROWS, :] + acc[t, ROWS : 2 * ROWS, :]) / jnp.maximum(
                acc[t, 2 * ROWS : 3 * ROWS, :] + acc[t, 3 * ROWS : 4 * ROWS, :], 1.0
            )
            for half in range(2):
                rows = pl.ds(SIDE * t + half, ROWS, stride=2)
                current[rows, :] = current[rows, :] + change[:, LANES * half : LANES * (half + 1)]
        if it + 1 < ITERS:
            table[...] = current[...].astype(jnp.bfloat16).astype(jnp.float32)

    sky_out[...] = current[...]
    for l in range(DETECTORS_LOCAL):
        base_out[l] = baseline[l : l + 1, 0:BASELINE_COUNT]

    wait_bytes(send_i, groups - 1, sent.at[0])
    wait_bytes(send_s, groups - 1, sent.at[1])
    for it in range(ITERS):
        base_sem = 2 + 6 * it
        wait_bytes(send_a.at[it], groups - 1, sent.at[base_sem])
        wait_bytes(send_b.at[it], groups - 1, sent.at[base_sem + 1])
        wait_bytes(send_c.at[it], groups - 1, sent.at[base_sem + 2])
        wait_bytes(recv_d.at[it], blocks - 1, sent.at[base_sem + 3])
        wait_bytes(send_e.at[it], groups - 1, sent.at[base_sem + 4])
        wait_bytes(send_h.at[it], groups - 1, sent.at[base_sem + 5])


def local(detector_samples, pixels, crossings, lengths, mode_templates, mixing, sky_map):
    groups = lax.axis_size("det")
    blocks = lax.axis_size("tile")
    chunks = SAMP_DEV // LANES
    vmem = pl.BlockSpec(memory_space=pltpu.VMEM)
    hbm = pl.BlockSpec(memory_space=pltpu.HBM)
    f32, bf16, i32, i16 = jnp.float32, jnp.bfloat16, jnp.int32, jnp.int16
    dma = pltpu.SemaphoreType.DMA
    sky, fit = pl.pallas_call(
        functools.partial(kernel, groups, blocks),
        out_shape=(
            jax.ShapeDtypeStruct((TILE_DEV * SIDE, SIDE), f32),
            jax.ShapeDtypeStruct((DETECTORS_LOCAL, 1, BASELINE_COUNT), f32),
        ),
        in_specs=[hbm] * 7,
        out_specs=(vmem, vmem),
        scratch_shapes=[
            pltpu.SMEM((DETECTORS_LOCAL, 1, SEG_PER), i32),
            pltpu.SMEM((DETECTORS_LOCAL, 1, BASELINE_COUNT), i32),
            pltpu.VMEM((DETECTORS_LOCAL, SAMP_DEV), f32),
            pltpu.VMEM((DETECTORS_LOCAL, SAMP_DEV), i32),
            pltpu.VMEM((MODES, DETECTORS_LOCAL * groups), f32),
            pltpu.VMEM((MODES, MODES), f32),
            pltpu.VMEM((TILE_DEV * SIDE, SIDE), f32),
            pltpu.SMEM((groups,), i32),
            pltpu.VMEM((DETECTORS_LOCAL * chunks, LANES), i32),
            pltpu.VMEM((DETECTORS_LOCAL * chunks, LANES), f32),
            pltpu.VMEM((DETECTORS_LOCAL * chunks, LANES), i32),
            pltpu.VMEM((ENTRIES, HALF, LANES), i32),
            pltpu.VMEM((ENTRIES, HALF, LANES), f32),
            pltpu.VMEM((DETECTORS_LOCAL * chunks, LANES), f32),
            pltpu.VMEM((DETECTORS_LOCAL * chunks, LANES), f32),
            pltpu.VMEM((DETECTORS_LOCAL * groups, LANES), f32),
            pltpu.VMEM((2 * DETECTORS_LOCAL * groups, DETECTORS_LOCAL * groups), bf16),
            pltpu.VMEM((TILE_DEV * SIDE, SIDE), f32),
            pltpu.VMEM((TOGETHER, SIDE, SIDE), f32),
            pltpu.VMEM((MANY, TERMS, HALF, LANES), f32),
            pltpu.VMEM((TILE_DEV, TERMS * ROWS, COLS), f32),
            pltpu.VMEM((groups * HALF // LANES, LANES, LANES), i32),
            pltpu.VMEM((groups, COLS // LANES, PART, LANES), bf16),
            pltpu.VMEM((groups, HALF, ROWS, LANES), bf16),
            pltpu.VMEM((groups, HALF, LANES), i16),
            pltpu.VMEM((groups, HALF, LANES), i16),
            pltpu.VMEM((ENTRIES, HALF, LANES), i16),
            pltpu.VMEM((groups, HALF, LANES), i16),
            pltpu.VMEM((groups, HALF, LANES), i16),
            pltpu.VMEM((groups, HALF, LANES), i32),
            pltpu.VMEM((ITERS, groups, HALF, LANES), bf16),
            pltpu.VMEM((ITERS, groups, HALF, LANES), bf16),
            pltpu.VMEM((ITERS, chunks, DETECTORS_LOCAL, LANES), f32),
            pltpu.VMEM((ITERS, groups, DETECTORS_LOCAL, LANES), f32),
            pltpu.VMEM((ITERS, groups, DETECTORS_LOCAL, LANES), f32),
            pltpu.VMEM((ITERS, chunks, DETECTORS_LOCAL, LANES), f32),
            pltpu.VMEM((ITERS, 8, LANES), f32),
            pltpu.VMEM((ITERS, blocks, 8, LANES), f32),
            pltpu.VMEM((ITERS, groups, HALF, LANES), f32),
            pltpu.VMEM((ITERS, groups, HALF, LANES), f32),
            pltpu.VMEM((DETECTORS_LOCAL, 1, LANES), f32),
            pltpu.VMEM((ITERS, groups, 1, LANES), f32),
            pltpu.VMEM((ITERS, groups, 1, LANES), f32),
            dma((7,)),
            dma((2 + 6 * ITERS,)),
            dma((groups,)),
            dma,
            dma((ITERS,)),
            dma((ITERS,)),
            dma((ITERS,)),
            dma((ITERS,)),
            dma((ITERS, groups)),
            dma((ITERS, groups)),
        ],
        compiler_params=pltpu.CompilerParams(
            collective_id=0, has_side_effects=True, vmem_limit_bytes=VMEM_BYTES
        ),
    )(*(
        pltpu.with_memory_space_constraint(array, pltpu.HBM)
        for array in (
            crossings, lengths, detector_samples, pixels, mode_templates.T, mixing,
            sky_map.reshape(TILE_DEV * SIDE, SIDE),
        )
    ))
    return sky.reshape(TILE_DEV, SIDE, SIDE), fit


def solution(mesh):
    placed = (
        P("det", "tile"),
        P("det", "tile"),
        P("det", "tile", None),
        P("det", "tile", None),
        P(),
        P(),
        P(("det", "tile"), None, None),
    )
    return jax.shard_map(
        local,
        mesh=mesh,
        in_specs=placed,
        out_specs=(P(("det", "tile"), None, None), P("det", "tile", None)),
        check_vma=False,
    )
```

```python
import functools

import jax
import jax.numpy as jnp
from jax import lax
from jax.experimental import pallas as pl
from jax.experimental.pallas import tpu as pltpu
from jax.sharding import PartitionSpec as P

SIDE = 128
PIX = 16384
TILE_DEV = 2
MODES = 64
DETECTORS_LOCAL = 4
SAMP_DEV = 4096
SEG_PER = 4
BASELINE_COUNT = 16
ITERS = 2
PART = SAMP_DEV // SEG_PER
ENTRIES = DETECTORS_LOCAL * SEG_PER
LANES = 128
COLS = 256
ROWS = PIX // COLS
HALF = PART // LANES
TERMS = 4
TOGETHER = 4
MANY = 8
VMEM_BYTES = 32 * 1024 * 1024

HUBER = 1.345
EPS = 1e-05
MESH = pl.DeviceIdType.MESH
ZRING = 8


def kernel(
    groups,
    blocks,
    cross_hbm,
    len_hbm,
    det_hbm,
    pix_hbm,
    templ_hbm,
    mixing_hbm,
    sky_hbm,
    sky_out,
    base_out,
    cross_ref,
    len_ref,
    det_ref,
    pix_ref,
    templ_ref,
    mixing_ref,
    current,
    ent_ref,
    code_h,
    det_h,
    seg_h,
    code_e,
    val_e,
    work,
    clean_h,
    stack,
    matrix,
    table,
    chosen,
    parts,
    acc,
    columns,
    coloh,
    rowoh,
    send_i,
    recv_i,
    seg_e,
    send_s,
    recv_s,
    code_g,
    send_a,
    recv_a,
    send_b,
    recv_b,
    send_c,
    recv_c,
    send_d,
    recv_d,
    send_e,
    recv_e,
    head,
    send_h,
    recv_h,
    load_sem,
    sent,
    sem_i,
    sem_s,
    sem_a,
    sem_b,
    sem_c,
    sem_d,
    sem_e,
    sem_h,
):
    me = lax.axis_index("det")
    block = lax.axis_index("tile")
    chunks = SAMP_DEV // LANES
    detectors = groups * DETECTORS_LOCAL
    xring = groups // ZRING
    my_x, my_z = lax.div(me, ZRING), lax.rem(me, ZRING)

    loads = [
        pltpu.make_async_copy(src, dst, load_sem.at[i])
        for i, (src, dst) in enumerate(
            ((cross_hbm, cross_ref), (pix_hbm, pix_ref), (len_hbm, len_ref), (det_hbm, det_ref),
             (templ_hbm, templ_ref), (mixing_hbm, mixing_ref), (sky_hbm, current))
        )
    ]
    for load in loads:
        load.start()

    def hops(dx, dz):
        return min(dx, xring - dx) + min(dz, ZRING - dz)

    xs = [lax.rem(my_x + dx, xring) * ZRING for dx in range(xring)]
    zs = [lax.rem(my_z + dz, ZRING) for dz in range(ZRING)]
    offsets = sorted(
        ((dx, dz) for dx in range(xring) for dz in range(ZRING) if dx or dz), key=lambda o: hops(*o)
    )
    near = [xs[dx] + zs[dz] for dx, dz in offsets]
    far = near[::-1]

    def copy_to(src, dst, send_sem, recv_sem, **place):
        return pltpu.make_async_remote_copy(
            src_ref=src, dst_ref=dst, send_sem=send_sem, recv_sem=recv_sem,
            device_id=place, device_id_type=MESH,
        )

    def wait_bytes(ref, count, sem):
        view = ref.at[pl.ds(0, count)]
        pltpu.make_async_copy(view, view, sem).wait()

    barrier = pltpu.get_barrier_semaphore()
    for o in far:
        pl.semaphore_signal(barrier, inc=1, device_id={"det": o}, device_id_type=MESH)
    others = [lax.rem(block + step, blocks) for step in range(1, blocks)]
    for b in others:
        pl.semaphore_signal(barrier, inc=1, device_id={"tile": b}, device_id_type=MESH)

    loads[0].wait()
    def entry_place(e):
        return e // SEG_PER, e % SEG_PER

    tiles = [cross_ref[entry_place(e)[0], 0, entry_place(e)[1]] for e in range(ENTRIES)]
    owners = [lax.div(tile, TILE_DEV * blocks) for tile in tiles]

    def find_entry(o, carry):
        found = jnp.int32(-1)
        for e in range(ENTRIES):
            found = jnp.where(owners[e] == o, e, found)
        ent_ref[o] = found
        return carry

    lax.fori_loop(0, groups, find_entry, 0)

    def rows_of(j):
        return slice(DETECTORS_LOCAL * j, DETECTORS_LOCAL * (j + 1))

    loads[1].wait()
    for j in range(chunks):
        code_h[rows_of(j), :] = pix_ref[:, LANES * j : LANES * (j + 1)]

    loads[2].wait()
    home = (chunks * DETECTORS_LOCAL // 8, 8, LANES)
    flat = (chunks * DETECTORS_LOCAL, LANES)
    sublane = lax.broadcasted_iota(jnp.int32, (8, LANES), 0)
    position = (
        lax.broadcasted_iota(jnp.int32, home, 0) * (8 // DETECTORS_LOCAL)
        + lax.div(lax.broadcasted_iota(jnp.int32, home, 1), DETECTORS_LOCAL)
    ) * LANES + lax.broadcasted_iota(jnp.int32, home, 2)
    ends = [jnp.int32(0)] * DETECTORS_LOCAL
    seg = jnp.zeros(home, jnp.int32)
    for n in range(BASELINE_COUNT):
        end = jnp.zeros((8, LANES), jnp.int32)
        for l in range(DETECTORS_LOCAL):
            ends[l] = ends[l] + len_ref[l, 0, n]
            end = jnp.where(lax.rem(sublane, DETECTORS_LOCAL) == l, ends[l], end)
        seg += (position >= end[None]).astype(jnp.int32)
    seg_h[...] = seg.reshape(flat)

    def fold(tile):
        turned = jnp.concatenate([tile[DETECTORS_LOCAL:], tile[:DETECTORS_LOCAL]], axis=0)
        return tile + turned

    def entry_rows(e):
        l, k = entry_place(e)
        return pl.ds(DETECTORS_LOCAL * HALF * k + l, HALF, stride=DETECTORS_LOCAL)

    for e in range(ENTRIES):
        code_e[e] = (
            code_h[entry_rows(e), :]
            + lax.rem(tiles[e], TILE_DEV) * PIX
        )
        seg_e[e] = seg_h[entry_rows(e), :].astype(jnp.int16)

    def pack_codes(o, carry):
        e = ent_ref[o]
        rows = code_e[jnp.maximum(e, 0)]
        send_i[o] = jnp.where(jnp.full(rows.shape, e, jnp.int32) >= 0, rows, -1).astype(jnp.int16)
        return carry

    lax.fori_loop(0, groups, pack_codes, 0)
    recv_i[me] = send_i[me]
    for load in loads[3:]:
        load.wait()

    pl.semaphore_wait(barrier, groups - 1 + blocks - 1)
    for o in near:
        copy_to(send_i.at[o], recv_i.at[me], sent.at[0], sem_i.at[me], det=o).start()

    for o in near:
        send_s[o] = seg_e[jnp.maximum(ent_ref[o], 0)]
        copy_to(send_s.at[o], recv_s.at[me], sent.at[1], sem_s, det=o).start()
    recv_s[me] = seg_e[jnp.maximum(ent_ref[me], 0)]

    for j in range(chunks):
        det_h[rows_of(j), :] = det_ref[:, LANES * j : LANES * (j + 1)]
    table[...] = current[...].astype(jnp.bfloat16).astype(jnp.float32)
    templates = templ_ref[...].T
    mixed = jnp.dot(
        templates, mixing_ref[...],
        precision=lax.Precision.HIGHEST, preferred_element_type=jnp.float32,
    )
    whole = jnp.dot(
        mixed, templ_ref[...],
        precision=lax.Precision.HIGHEST, preferred_element_type=jnp.float32,
    )
    high = whole.astype(jnp.bfloat16)
    matrix[0:detectors, :] = high
    matrix[detectors:, :] = (whole - high.astype(jnp.float32)).astype(jnp.bfloat16)
    def turn_columns():
        column = jnp.bitwise_and(code_g[...].reshape(groups * HALF, LANES), COLS - 1).T
        for part in range(groups * HALF // LANES):
            columns[part] = column[:, LANES * part : LANES * (part + 1)]

    def flags(part, first, last):
        def one(i, carry):
            d = LANES // HALF * part + i
            code = code_g[d]
            row = jnp.where(
                code < 0, -1, jnp.bitwise_and(lax.shift_right_arithmetic(code, 8), ROWS - 1)
            )
            square = (LANES, LANES)
            lane = lax.broadcasted_iota(jnp.int32, square, 1)
            for q in range(HALF):
                rowoh[d, q] = (
                    jnp.broadcast_to(row[q : q + 1, :], (ROWS, LANES))
                    == lax.broadcasted_iota(jnp.int32, (ROWS, LANES), 0)
                ).astype(jnp.float32).astype(jnp.bfloat16)
                col = jnp.take_along_axis(
                    columns[part], jnp.full(square, HALF * i + q, jnp.int32), axis=1
                )
                for h in range(COLS // LANES):
                    coloh[d, h, LANES * q : LANES * (q + 1), :] = (
                        col == lane + LANES * h
                    ).astype(jnp.float32).astype(jnp.bfloat16)
            return carry

        lax.fori_loop(first, last, one, 0)

    def zigzag(i, size):
        return size // 2 + lax.div(i + 1, 2) * (1 - 2 * lax.rem(i, 2))

    def far_peer(step):
        x = lax.rem(my_x + zigzag(lax.rem(step, xring), xring), xring)
        z = lax.rem(my_z + zigzag(lax.div(step, xring), ZRING), ZRING)
        return x * ZRING + z

    def near_peer(step):
        return far_peer(groups - 1 - step)

    baseline = jnp.zeros((8, LANES), jnp.float32)

    for it in range(ITERS):
        base_sem = 2 + 6 * it

        def answer(batch, carry):
            slots = [
                near_peer(step) if it == 0 else far_peer(step)
                for step in (TOGETHER * batch + i for i in range(TOGETHER))
            ]
            if it == 0:
                for i, d in enumerate(slots):
                    @pl.when(TOGETHER * batch + i > 0)
                    def _():
                        copy_to(
                            send_i.at[d], recv_i.at[d], sent.at[0], sem_i.at[d], det=d
                        ).wait_recv()
            values = []
            for i, d in enumerate(slots):
                if it == 0:
                    code_g[d] = recv_i[d].astype(jnp.int32)
                code = code_g[d]
                row = jnp.bitwise_and(lax.shift_right_arithmetic(code, 7), SIDE - 1)
                col = jnp.bitwise_and(code, LANES - 1)
                second = jnp.bitwise_and(code, PIX) > 0
                for g in range(SIDE // 8):
                    chosen[i, 8 * g : 8 * g + 8, :] = jnp.where(
                        second,
                        table[SIDE + 8 * g : SIDE + 8 * g + 8, :],
                        table[8 * g : 8 * g + 8, :],
                    )
                value = jnp.zeros((HALF, LANES), jnp.float32)
                for r in range(SIDE):
                    line = jnp.broadcast_to(chosen[i, r : r + 1, :], (HALF, LANES))
                    value = jnp.where(row == r, jnp.take_along_axis(line, col, axis=1), value)
                values.append(value)
            for d, value in zip(slots, values):
                send_a[it, d] = value.astype(jnp.bfloat16)
            for d in slots:
                @pl.when(d != me)
                def _():
                    copy_to(
                        send_a.at[it, d], recv_a.at[it, me], sent.at[base_sem], sem_a.at[it], det=d
                    ).start()

            return carry

        lax.fori_loop(0, groups // TOGETHER, answer, 0)
        recv_a[it, me] = send_a[it, me]
        if it == 0:
            turn_columns()
            flags(0, 0, 8)
        wait_bytes(recv_a.at[it], groups - 1, sem_a.at[it])

        for e in range(ENTRIES):
            work[entry_rows(e), :] = recv_a[it, owners[e]].astype(jnp.float32)
        residual = det_h[...] - work[...]
        for j in range(chunks):
            send_b[it, j] = residual[rows_of(j), :]
        recv_b[it, me] = send_b[it, me]
        for j in far:
            copy_to(
                send_b.at[it, j], recv_b.at[it, me], sent.at[base_sem + 1], sem_b.at[it], det=j
            ).start()
        if it == 0:
            flags(0, 8, 16)
            flags(1, 0, 4)
        wait_bytes(recv_b.at[it], groups - 1, sem_b.at[it])

        for d in range(groups):
            stack[rows_of(d), :] = recv_b[it, d]
        every = stack[...]
        high = every.astype(jnp.bfloat16)
        low = (every - high.astype(jnp.float32)).astype(jnp.bfloat16)
        both = jnp.dot(matrix[...], high, preferred_element_type=jnp.float32)
        every = every - (
            both[0:detectors, :]
            + both[detectors:, :]
            + jnp.dot(matrix[0:detectors, :], low, preferred_element_type=jnp.float32)
        )
        for d in range(groups):
            send_c[it, d] = every[rows_of(d), :]
        recv_c[it, me] = send_c[it, me]
        for d in far:
            copy_to(
                send_c.at[it, d], recv_c.at[it, me], sent.at[base_sem + 2], sem_c.at[it], det=d
            ).start()
        acc[...] = jnp.zeros_like(acc)
        if it == 0:
            flags(1, 4, 16)
        wait_bytes(recv_c.at[it], groups - 1, sem_c.at[it])

        for j in range(chunks):
            clean_h[rows_of(j), :] = recv_c[it, j]
        cleaned = clean_h[...].reshape(home)
        send_d[it] = jnp.sum(cleaned * cleaned, axis=0)
        recv_d[it, block] = send_d[it]
        for b in others:
            copy_to(
                send_d.at[it], recv_d.at[it, block], sent.at[base_sem + 3], sem_d.at[it], tile=b
            ).start()
        for e in range(ENTRIES):
            val_e[e] = clean_h[entry_rows(e), :]
        for o in near:
            send_e[it, o] = val_e[jnp.maximum(ent_ref[o], 0)]
            copy_to(
                send_e.at[it, o], recv_e.at[it, me], sent.at[base_sem + 4], sem_e.at[it, me], det=o
            ).start()
        recv_e[it, me] = val_e[jnp.maximum(ent_ref[me], 0)]
        wait_bytes(recv_d.at[it], blocks - 1, sem_d.at[it])
        squares = fold(jnp.sum(recv_d[it], axis=0))
        squares = jnp.sum(squares, axis=1, keepdims=True)
        level = HUBER * jnp.sqrt(squares / (SAMP_DEV * blocks) + EPS)
        weight = level[None] / jnp.maximum(jnp.abs(cleaned), level[None])
        weighted = weight * cleaned
        seg = seg_h[...].reshape(home)
        lane = lax.broadcasted_iota(jnp.int32, (8, LANES), 1)
        numerator = jnp.zeros((8, LANES), jnp.float32)
        denominator = jnp.zeros((8, LANES), jnp.float32)
        for n in range(BASELINE_COUNT):
            inside = seg == n
            numerator = jnp.where(
                lane == n,
                jnp.sum(jnp.sum(jnp.where(inside, weighted, 0.0), axis=0), axis=1, keepdims=True),
                numerator,
            )
            denominator = jnp.where(
                lane == n,
                jnp.sum(jnp.sum(jnp.where(inside, weight, 0.0), axis=0), axis=1, keepdims=True),
                denominator,
            )
        denominator = fold(denominator)
        increment = fold(numerator) / jnp.where(denominator > 0.0, denominator, 1.0)
        line = jnp.where(lane == BASELINE_COUNT, level, increment)
        for l in range(DETECTORS_LOCAL):
            head[l] = line[l : l + 1, :]
        for o in near:
            send_h[it, o] = head[lax.div(jnp.maximum(ent_ref[o], 0), SEG_PER)]
            copy_to(
                send_h.at[it, o], recv_h.at[it, me], sent.at[base_sem + 5], sem_h.at[it, me], det=o
            ).start()
        recv_h[it, me] = head[lax.div(jnp.maximum(ent_ref[me], 0), SEG_PER)]
        baseline = baseline + increment
        if it + 1 < ITERS:
            stepped = jnp.zeros(home, jnp.float32)
            for n in range(BASELINE_COUNT):
                stepped = jnp.where(seg == n, increment[:, n : n + 1][None], stepped)
            det_h[...] = det_h[...] - stepped.reshape(flat)

        if it == 0:
            wait_bytes(recv_s, groups - 1, sem_s)

        def collect(first, count):
            slots = [near_peer(first + i) for i in range(count)]
            for i, d in enumerate(slots):
                @pl.when(d != me)
                def _():
                    copy_to(
                        send_e.at[it, d], recv_e.at[it, d], sent.at[base_sem + 4], sem_e.at[it, d],
                        det=d,
                    ).wait_recv()
                    copy_to(
                        send_h.at[it, d], recv_h.at[it, d], sent.at[base_sem + 5], sem_h.at[it, d],
                        det=d,
                    ).wait_recv()
            for i, d in enumerate(slots):
                cleaned_d = recv_e[it, d]
                line = jnp.broadcast_to(recv_h[it, d], (HALF, LANES))
                seg_d = recv_s[d].astype(jnp.int32)
                step_d = jnp.take_along_axis(line, seg_d, axis=1)
                level_d = jnp.take_along_axis(
                    line, jnp.full((HALF, LANES), BASELINE_COUNT, jnp.int32), axis=1
                )
                weight_d = level_d / jnp.maximum(jnp.abs(cleaned_d), level_d)
                value_d = weight_d * (cleaned_d - step_d)
                high = value_d.astype(jnp.bfloat16).astype(jnp.float32)
                parts[i, 0] = high
                parts[i, 1] = value_d - high
                high = weight_d.astype(jnp.bfloat16).astype(jnp.float32)
                parts[i, 2] = high
                parts[i, 3] = weight_d - high
            sums = []
            for i, d in enumerate(slots):
                weighed = jnp.concatenate(
                    [
                        jnp.concatenate(
                            [
                                rowoh[d, q]
                                * jnp.broadcast_to(
                                    parts[i, t, q : q + 1, :], (ROWS, LANES)
                                ).astype(jnp.bfloat16)
                                for t in range(TERMS)
                            ],
                            axis=0,
                        )
                        for q in range(HALF)
                    ],
                    axis=1,
                )
                spread = jnp.concatenate([coloh[d, h] for h in range(COLS // LANES)], axis=1)
                product = jnp.dot(weighed, spread, preferred_element_type=jnp.float32)
                product = jnp.concatenate(
                    [
                        product[2 * t * ROWS : (2 * t + 1) * ROWS, :]
                        + product[(2 * t + 1) * ROWS : (2 * t + 2) * ROWS, :]
                        for t in range(TERMS // 2)
                    ],
                    axis=0,
                )
                second = (
                    jnp.broadcast_to(jnp.bitwise_and(code_g[d], PIX)[0:1, 0:1], product.shape) > 0
                )
                sums.append((jnp.where(second, 0.0, product), jnp.where(second, product, 0.0)))
            for t in range(TILE_DEV):
                total = sums[0][t]
                for part in sums[1:]:
                    total = total + part[t]
                acc[t] += total

        def collect_many(batch, carry):
            collect(TOGETHER + MANY * batch, MANY)
            return carry

        collect(0, TOGETHER)
        many = (groups - TOGETHER) // MANY
        lax.fori_loop(0, many, collect_many, 0)
        rest = TOGETHER + MANY * many
        if rest < groups:
            collect(rest, groups - rest)
        for t in range(TILE_DEV):
            change = acc[t, 0:ROWS, :] / jnp.maximum(acc[t, ROWS : 2 * ROWS, :], 1.0)
            for half in range(2):
                rows = pl.ds(SIDE * t + half, ROWS, stride=2)
                current[rows, :] = current[rows, :] + change[:, LANES * half : LANES * (half + 1)]
        if it + 1 < ITERS:
            table[...] = current[...].astype(jnp.bfloat16).astype(jnp.float32)

    sky_out[...] = current[...]
    for l in range(DETECTORS_LOCAL):
        base_out[l] = baseline[l : l + 1, 0:BASELINE_COUNT]

    wait_bytes(send_i, groups - 1, sent.at[0])
    wait_bytes(send_s, groups - 1, sent.at[1])
    for it in range(ITERS):
        base_sem = 2 + 6 * it
        wait_bytes(send_a.at[it], groups - 1, sent.at[base_sem])
        wait_bytes(send_b.at[it], groups - 1, sent.at[base_sem + 1])
        wait_bytes(send_c.at[it], groups - 1, sent.at[base_sem + 2])
        wait_bytes(recv_d.at[it], blocks - 1, sent.at[base_sem + 3])
        wait_bytes(send_e.at[it], groups - 1, sent.at[base_sem + 4])
        wait_bytes(send_h.at[it], groups - 1, sent.at[base_sem + 5])


def local(detector_samples, pixels, crossings, lengths, mode_templates, mixing, sky_map):
    groups = lax.axis_size("det")
    blocks = lax.axis_size("tile")
    chunks = SAMP_DEV // LANES
    vmem = pl.BlockSpec(memory_space=pltpu.VMEM)
    hbm = pl.BlockSpec(memory_space=pltpu.HBM)
    f32, bf16, i32, i16 = jnp.float32, jnp.bfloat16, jnp.int32, jnp.int16
    dma = pltpu.SemaphoreType.DMA
    sky, fit = pl.pallas_call(
        functools.partial(kernel, groups, blocks),
        out_shape=(
            jax.ShapeDtypeStruct((TILE_DEV * SIDE, SIDE), f32),
            jax.ShapeDtypeStruct((DETECTORS_LOCAL, 1, BASELINE_COUNT), f32),
        ),
        in_specs=[hbm] * 7,
        out_specs=(vmem, vmem),
        scratch_shapes=[
            pltpu.SMEM((DETECTORS_LOCAL, 1, SEG_PER), i32),
            pltpu.SMEM((DETECTORS_LOCAL, 1, BASELINE_COUNT), i32),
            pltpu.VMEM((DETECTORS_LOCAL, SAMP_DEV), f32),
            pltpu.VMEM((DETECTORS_LOCAL, SAMP_DEV), i32),
            pltpu.VMEM((MODES, DETECTORS_LOCAL * groups), f32),
            pltpu.VMEM((MODES, MODES), f32),
            pltpu.VMEM((TILE_DEV * SIDE, SIDE), f32),
            pltpu.SMEM((groups,), i32),
            pltpu.VMEM((DETECTORS_LOCAL * chunks, LANES), i32),
            pltpu.VMEM((DETECTORS_LOCAL * chunks, LANES), f32),
            pltpu.VMEM((DETECTORS_LOCAL * chunks, LANES), i32),
            pltpu.VMEM((ENTRIES, HALF, LANES), i32),
            pltpu.VMEM((ENTRIES, HALF, LANES), f32),
            pltpu.VMEM((DETECTORS_LOCAL * chunks, LANES), f32),
            pltpu.VMEM((DETECTORS_LOCAL * chunks, LANES), f32),
            pltpu.VMEM((DETECTORS_LOCAL * groups, LANES), f32),
            pltpu.VMEM((2 * DETECTORS_LOCAL * groups, DETECTORS_LOCAL * groups), bf16),
            pltpu.VMEM((TILE_DEV * SIDE, SIDE), f32),
            pltpu.VMEM((TOGETHER, SIDE, SIDE), f32),
            pltpu.VMEM((MANY, TERMS, HALF, LANES), f32),
            pltpu.VMEM((TILE_DEV, TERMS // 2 * ROWS, COLS), f32),
            pltpu.VMEM((groups * HALF // LANES, LANES, LANES), i32),
            pltpu.VMEM((groups, COLS // LANES, PART, LANES), bf16),
            pltpu.VMEM((groups, HALF, ROWS, LANES), bf16),
            pltpu.VMEM((groups, HALF, LANES), i16),
            pltpu.VMEM((groups, HALF, LANES), i16),
            pltpu.VMEM((ENTRIES, HALF, LANES), i16),
            pltpu.VMEM((groups, HALF, LANES), i16),
            pltpu.VMEM((groups, HALF, LANES), i16),
            pltpu.VMEM((groups, HALF, LANES), i32),
            pltpu.VMEM((ITERS, groups, HALF, LANES), bf16),
            pltpu.VMEM((ITERS, groups, HALF, LANES), bf16),
            pltpu.VMEM((ITERS, chunks, DETECTORS_LOCAL, LANES), f32),
            pltpu.VMEM((ITERS, groups, DETECTORS_LOCAL, LANES), f32),
            pltpu.VMEM((ITERS, groups, DETECTORS_LOCAL, LANES), f32),
            pltpu.VMEM((ITERS, chunks, DETECTORS_LOCAL, LANES), f32),
            pltpu.VMEM((ITERS, 8, LANES), f32),
            pltpu.VMEM((ITERS, blocks, 8, LANES), f32),
            pltpu.VMEM((ITERS, groups, HALF, LANES), f32),
            pltpu.VMEM((ITERS, groups, HALF, LANES), f32),
            pltpu.VMEM((DETECTORS_LOCAL, 1, LANES), f32),
            pltpu.VMEM((ITERS, groups, 1, LANES), f32),
            pltpu.VMEM((ITERS, groups, 1, LANES), f32),
            dma((7,)),
            dma((2 + 6 * ITERS,)),
            dma((groups,)),
            dma,
            dma((ITERS,)),
            dma((ITERS,)),
            dma((ITERS,)),
            dma((ITERS,)),
            dma((ITERS, groups)),
            dma((ITERS, groups)),
        ],
        compiler_params=pltpu.CompilerParams(
            collective_id=0, has_side_effects=True, vmem_limit_bytes=VMEM_BYTES
        ),
    )(*(
        pltpu.with_memory_space_constraint(array, pltpu.HBM)
        for array in (
            crossings, lengths, detector_samples, pixels, mode_templates.T, mixing,
            sky_map.reshape(TILE_DEV * SIDE, SIDE),
        )
    ))
    return sky.reshape(TILE_DEV, SIDE, SIDE), fit


def solution(mesh):
    placed = (
        P("det", "tile"),
        P("det", "tile"),
        P("det", "tile", None),
        P("det", "tile", None),
        P(),
        P(),
        P(("det", "tile"), None, None),
    )
    return jax.shard_map(
        local,
        mesh=mesh,
        in_specs=placed,
        out_specs=(P(("det", "tile"), None, None), P("det", "tile", None)),
        check_vma=False,
    )
```
